128 devices in a mesh: req: 128 (over z, y, x, core).
Axes of the slice: x: 4, y: 4, z: 4, core: 2. Of those that a mesh axis runs over, the one named last changes fastest.
Arguments:
- queries: bfloat16 [16384, 2560], P('req'), may hold values from -8 to 8
- prefix_keys: bfloat16 [32768, 640], P('req'), may hold values from -6 to 6
- prefix_values: bfloat16 [32768, 640], P('req'), may hold values from -6 to 6
- pool_keys: bfloat16 [16384, 16, 640], P('req'), may hold values from -6 to 6
- pool_values: bfloat16 [16384, 16, 640], P('req'), may hold values from -6 to 6
- page_table: int32 [16384, 8], P('req'), may hold values from 0 to 127
- private_length: int32 [16384], P('req'), may hold values from 1 to 128
- group_ids: int32 [16384, 1], P('req'), may hold values from 0 to 127; in each aligned block of 128 rows (0 to 127, 128 to 255, ...) at most 2 rows name the same one
- live_rows: int32 [128], P('req'), may hold values from 1 to 128, 8192 in all
- out_weight: bfloat16 [2560, 2560], replicated, may hold values from -0.75 to 0.75
Outputs:
- projected: bfloat16 [16384, 2560], P('req')
The draws below stay inside these ranges and needn't reach their ends.
Inputs may be any that keep to these rules, and one draw needn't show every extreme that they name: `group_ids`: the group of a row is also the index of the device that holds that group's prompt; at most 2 rows of one device name one group. `live_rows`: the counts sum to 8192.
All inputs are finite; a program needn't handle non-finite values. No bound on the sum of `live_rows` on one device may be relied on, other than what follows from the above.
Results may differ from the reference program's by a relative error of at most 0.007.
Values may be sent and summed in bfloat16 or wider, within the bound.
A program may use at most 128 MiB of HBM per device.

```python
import math
import jax
import jax.numpy as jnp
import numpy as np
from jax import lax

D = 2560
H = 32
KVH = 8
HD = 80
Q_DEV = 128
PREF = 256
PAGE = 16
MAXP = 8
POOL = 128
KW = 640
GROUPS = 128
ROWS = 16384
PREFS = 32768
POOLS = 16384
PRIV = 128
GMOST = 2
BAL = 64
N_REQ = 128


def draw_queries(key, part):
    normal_part = jnp.clip(jax.random.normal(jax.random.fold_in(key, 11), (ROWS, D), jnp.float32), -6.0, 6.0)
    return normal_part.astype(jnp.bfloat16)


def draw_prefix_keys(key, part):
    normal_part = jnp.clip(jax.random.normal(jax.random.fold_in(key, 21), (PREFS, KW), jnp.float32), -6.0, 6.0)
    return normal_part.astype(jnp.bfloat16)


def draw_pool_keys(key, part):
    normal_part = jnp.clip(jax.random.normal(jax.random.fold_in(key, 31), (POOLS, PAGE, KW), jnp.float32), -6.0, 6.0)
    return normal_part.astype(jnp.bfloat16)


def with_ends(result, own_key, smallest, top_value):
    shape = result.shape
    spot = [jax.random.randint(jax.random.fold_in(own_key, axis), (), 0, shape[axis]) for axis in range(len(shape))]
    result = result.at[tuple(spot)].set(smallest)
    longest = shape.index(max(shape))
    spot[longest] = (spot[longest] + 1) % shape[longest]
    return result.at[tuple(spot)].set(top_value)


def steps_of(key, dims, split, least, high):
    factor_of = 1.0
    for dim, parts in split:
        steps = jax.random.uniform(jax.random.fold_in(jax.random.fold_in(key, 6), dim), (parts,), jnp.float32, least / len(split), high / len(split))
        factor_of = factor_of * jnp.repeat(jnp.exp(steps), dims[dim] // parts).reshape((-1,) + (1,) * (len(dims) - 1 - dim))
    return factor_of


def profile(count, total, reach, skew):
    weights = [(1 << 20) // math.isqrt(grade ** skew) + 1 for grade in range(2, count + 1)]
    rest, holding = total - reach - (count - 1), [1] * (count - 1)
    while rest > 0:
        free = [i for i in range(count - 1) if holding[i] < reach]
        whole, left = sum([weights[i] for i in free]), rest
        for i in free:
            more = min(reach - holding[i], max(1, left * weights[i] // whole), rest)
            holding[i] = holding[i] + more
            rest = rest - more
    return np.array([reach] + holding)


def uneven(rng, number_of, total, reach, lean):
    if number_of == 2:
        one = jax.random.randint(rng, (), max(1, total - reach), min(reach, total - 1) + 1)
        return jnp.stack([one, total - one])
    sizes = jnp.asarray(profile(number_of, total, reach, lean), jnp.int32)
    pairs = (number_of - 1) // 2
    source_of, receiver = sizes[1:1 + 2 * pairs:2], sizes[2:2 + 2 * pairs:2]
    room = jnp.minimum(source_of - 1, reach - receiver)
    moved = jax.random.randint(jax.random.fold_in(rng, 1), (pairs,), 0, 1 << 20) % (room + 1)
    sizes = sizes.at[1:1 + 2 * pairs:2].set(source_of - moved).at[2:2 + 2 * pairs:2].set(receiver + moved)
    return sizes[jax.random.permutation(jax.random.fold_in(rng, 2), number_of)]


def deal_out(rng, own, number, rows, number_of, top, reach, skew):
    order = jax.random.permutation(rng, number_of)
    heavy_load, usual = shares(number_of, rows * top, reach, skew, True), shares(number_of, rows * top, reach, skew, False)
    places = jnp.arange(number_of)

    def named(sizes, offset_by):
        used = int((sizes > 0).sum())
        fixed = max(1, used // 4)
        passed = fixed + (places - fixed + offset_by * (used - fixed)) % max(1, number_of - fixed)
        return jnp.zeros((number_of,), jnp.int32).at[order[jnp.where(places < fixed, places, passed)]].set(jnp.asarray(sizes, jnp.int32))

    sizes = jnp.where(number % 4 == 0, named(heavy_load, number // 4), named(usual, number - number // 4 - 1))
    mixed = jax.random.permutation(jax.random.fold_in(own, 3), number_of)
    source_of, taker = mixed[0:number_of // 2 * 2:2], mixed[1:number_of // 2 * 2:2]
    margin = jnp.minimum(sizes[source_of] - 1, reach - sizes[taker]) // 2
    margin = jnp.where((source_of == order[0]) | (taker == order[0]) | (sizes[taker] == 0), 0, jnp.maximum(margin, 0))
    passed = jax.random.randint(jax.random.fold_in(own, 4), (number_of // 2,), 0, 1 << 20) % (margin + 1)
    sizes = sizes.at[source_of].add(-passed).at[taker].add(passed)
    members = jnp.searchsorted(jnp.cumsum(sizes), jnp.arange(rows * top), side="right").astype(jnp.int32)
    listing = members.reshape(top, rows).T
    listing = listing[jax.random.permutation(jax.random.fold_in(own, 1), rows)]
    offset_by = jax.random.randint(jax.random.fold_in(own, 2), (rows, 1), 0, top)
    return jnp.take_along_axis(listing, (jnp.arange(top)[None, :] + offset_by) % top, axis=1)


def shares(number_of, total, bound, skew, full):
    portions = [(1 << 20) // math.isqrt(grade ** skew) + 1 for grade in range(1, number_of + 1)]
    largest = bound if full else min(bound, max(-(-total // number_of), total * portions[0] // sum(portions)))
    least = 1 if total - largest >= number_of - 1 else 0
    counts, spare = [largest] + [least] * (number_of - 1), total - largest - least * (number_of - 1)
    while spare > 0:
        candidates = [i for i in range(1, number_of) if counts[i] < largest] or [i for i in range(1, number_of) if counts[i] < bound]
        pool, remaining = sum([portions[i] for i in candidates]), spare
        for i in candidates:
            more = min(bound - counts[i], max(1, remaining * portions[i] // pool), spare)
            counts[i] = counts[i] + more
            spare = spare - more
    return np.array(counts)


def normal_values(key, extent, spread, most, shards=(), held_as=jnp.bfloat16):
    values = jax.random.normal(key, extent, jnp.float32) * spread
    if len(shards) > 0:
        values = steps_of(key, extent, shards, -0.22, 0.18) * values
    return jnp.clip(values, min=-most, max=most).astype(held_as)


def setup_inputs(seed: int = 0) -> dict:
    seeds = jax.random.split(jax.random.key(seed), 11)
    queries = draw_queries(jax.random.fold_in(seeds[10], 71), 0)
    prefix_keys = draw_prefix_keys(jax.random.fold_in(seeds[10], 71), 0)
    prefix_values = normal_values(seeds[2], (PREFS, KW), 1.0, 6.0, ((0, 128),))
    pool_keys = draw_pool_keys(jax.random.fold_in(seeds[10], 71), 0)
    pool_values = normal_values(seeds[4], (POOLS, PAGE, KW), 1.0, 6.0, ((0, 128),))
    page_table = with_ends(jax.random.randint(seeds[5], (ROWS, MAXP), 0, POOL), jax.random.fold_in(seeds[5], 1), 0, POOL - 1).astype(jnp.int32)
    private_length = with_ends(jax.random.randint(seeds[6], (ROWS,), 1, PRIV + 1), jax.random.fold_in(seeds[6], 1), 1, PRIV).astype(jnp.int32)
    group_ids_keys = jax.random.split(jax.random.fold_in(seeds[7], 1), ROWS // Q_DEV)
    group_ids_turns = jax.random.permutation(jax.random.fold_in(seeds[7], 3), ROWS // Q_DEV)
    group_ids = jax.vmap(lambda own, number: deal_out(jax.random.fold_in(seeds[7], 2), own, number, Q_DEV, GROUPS, 1, GMOST, 2))(group_ids_keys, group_ids_turns).reshape((ROWS, 1))
    live_rows = uneven(seeds[8], N_REQ, N_REQ * BAL, Q_DEV, 2).astype(jnp.int32)
    out_weight = normal_values(seeds[9], (D, D), (D // 40) ** -0.5, 0.75)
    return {"queries": queries, "prefix_keys": prefix_keys, "prefix_values": prefix_values, "pool_keys": pool_keys, "pool_values": pool_values, "page_table": page_table, "private_length": private_length, "group_ids": group_ids, "live_rows": live_rows, "out_weight": out_weight}


def weigh(scores, values, spec):
    largest = jnp.max(scores, axis=-1, keepdims=True)
    weights = jnp.exp(scores - largest)
    weight_sum = jnp.sum(weights, axis=-1)
    rounded = lax.optimization_barrier(weights.astype(jnp.bfloat16)).astype(jnp.float32)
    summed = jnp.einsum(spec, rounded, values)
    return summed / weight_sum[..., None], largest[..., 0] + jnp.log(weight_sum)


def reference(queries, prefix_keys, prefix_values, pool_keys, pool_values, page_table, private_length, group_ids, live_rows, out_weight):
    block_rows = 32
    block_count = ROWS // block_rows
    group_size = H // KVH
    scale = HD ** -0.5
    prefix_table = prefix_keys.reshape(GROUPS, PREF, KVH, HD)
    prefix_store = prefix_values.reshape(GROUPS, PREF, KVH, HD)

    def one_block(block_index):
        first_row = block_index * block_rows
        query_block = lax.dynamic_slice_in_dim(queries, first_row, block_rows, 0).astype(jnp.float32)
        query_block = query_block.reshape(block_rows, KVH, group_size, HD)
        groups = lax.dynamic_slice_in_dim(group_ids[:, 0], first_row, block_rows, 0)
        key_rows = prefix_table[groups].astype(jnp.float32)
        value_rows = prefix_store[groups].astype(jnp.float32)
        scores = jnp.einsum("rkgd,rtkd->rkgt", query_block, key_rows) * scale
        prefix_out, prefix_lse = weigh(scores, value_rows, "rkgt,rtkd->rkgd")
        prefix_out = lax.optimization_barrier(prefix_out.astype(jnp.bfloat16)).astype(jnp.float32)
        device = (first_row // Q_DEV).astype(jnp.int32)
        page_rows = lax.dynamic_slice_in_dim(page_table, first_row, block_rows, 0) + device * POOL
        private_keys = pool_keys[page_rows].reshape(block_rows, PRIV, KVH, HD).astype(jnp.float32)
        private_values = pool_values[page_rows].reshape(block_rows, PRIV, KVH, HD).astype(jnp.float32)
        lengths = lax.dynamic_slice_in_dim(private_length, first_row, block_rows, 0)
        visible = jnp.arange(PRIV, dtype=jnp.int32)[None, :] < lengths[:, None]
        scores = jnp.einsum("rkgd,rtkd->rkgt", query_block, private_keys) * scale
        scores = jnp.where(visible[:, None, None, :], scores, -1e30)
        private_out, private_lse = weigh(scores, private_values, "rkgt,rtkd->rkgd")
        largest = jnp.maximum(prefix_lse, private_lse)
        prefix_share = jnp.exp(prefix_lse - largest)
        private_share = jnp.exp(private_lse - largest)
        combined = (prefix_share[..., None] * prefix_out + private_share[..., None] * private_out) / (prefix_share + private_share)[..., None]
        return combined.reshape(block_rows, D).astype(jnp.bfloat16)

    attended = lax.map(one_block, jnp.arange(block_count, dtype=jnp.int32)).reshape(ROWS, D)
    projected = jnp.dot(attended, out_weight, preferred_element_type=jnp.float32)
    row_index = jnp.arange(ROWS, dtype=jnp.int32)
    is_live = (row_index % Q_DEV) < live_rows[row_index // Q_DEV]
    return jnp.where(is_live[:, None], projected, 0.0).astype(jnp.bfloat16)
```

```python
import functools

import jax
import jax.numpy as jnp
from jax import lax
from jax.experimental import pallas as pl
from jax.experimental.pallas import tpu as pltpu
from jax.sharding import PartitionSpec as P

MESH = pl.DeviceIdType.MESH
H = 32
KVH = 8
HD = 80
GQ = H // KVH
KW = KVH * HD
LANES = 128
TILES = KW // LANES
SLOTS = 2
MIX = 45
CHUNKS = 4
BATCH = 8
SCALE = HD ** (-0.5)
LOG2E = 1.4426950408889634
NT = (((1,), (1,)), ((), ()))
NN = (((1,), (0,)), ((), ()))


def dot(a, b, dims=NN):
    return lax.dot_general(a, b, dims, preferred_element_type=jnp.float32)


def iota(shape, axis):
    return lax.broadcasted_iota(jnp.int32, shape, axis)


def window(k):
    first = k * HD // LANES
    last = (k * HD + HD - 1) // LANES
    return first, last + 1


def of_head(lane, k):
    return (lane >= k * HD) & (lane < (k + 1) * HD)


def kernel(
    n,
    rows,
    table,
    lengths,
    live,
    groups,
    q_hbm,
    pk_hbm,
    pv_hbm,
    poolk_hbm,
    poolv_hbm,
    w_hbm,
    o_ref,
    q_v,
    pk_v,
    pv_v,
    poolk,
    poolv,
    w_v,
    qp,
    qf,
    kpad,
    vpad,
    send,
    recv,
    result,
    back,
    stage,
    stat,
    own,
    own_lse,
    load_sem,
    send_sem,
    recv_sem,
    back_send_sem,
    back_sem,
):
    me = lax.axis_index("req")
    per = n // CHUNKS
    load_q = pltpu.make_async_copy(q_hbm, q_v, load_sem.at[0])
    load_pk = pltpu.make_async_copy(pk_hbm, pk_v, load_sem.at[1])
    load_pv = pltpu.make_async_copy(pv_hbm, pv_v, load_sem.at[2])
    load_poolk = pltpu.make_async_copy(poolk_hbm, poolk, load_sem.at[3])
    load_poolv = pltpu.make_async_copy(poolv_hbm, poolv, load_sem.at[4])
    load_q.start()
    barrier = pltpu.get_barrier_semaphore()

    def greet(i, c):
        pl.semaphore_signal(
            barrier, inc=1, device_id=(lax.rem(me + i, n),), device_id_type=MESH
        )
        return c

    lax.fori_loop(1, n, greet, 0)
    load_pk.start()
    load_pv.start()
    load_poolk.start()
    load_poolv.start()

    def load_w(b, c):
        source = (lax.rem(b, KVH) * GQ + b // KVH) * HD
        pltpu.make_async_copy(
            w_hbm.at[pl.ds(pl.multiple_of(source, 16), HD)],
            w_v.at[pl.ds(pl.multiple_of(b * HD, 16), HD)],
            load_sem.at[5],
        ).start()
        return c

    lax.fori_loop(0, H, load_w, 0)

    group_row = groups[...]
    eye = iota((rows, rows), 0) == iota((rows, rows), 1)
    group_col = jnp.sum(jnp.where(eye, group_row, 0), axis=1, keepdims=True)
    earlier = (group_col == group_row) & (iota((rows, rows), 0) < iota((rows, rows), 1))
    rank = jnp.sum(earlier.astype(jnp.int32), axis=0, keepdims=True)
    slot_row = group_row * SLOTS + rank
    slot_wide = jnp.concatenate([slot_row + j * (SLOTS * n) for j in range(GQ)], axis=1)
    index = iota((n * GQ * SLOTS, 1), 0)
    offset = index // (GQ * SLOTS)
    which = index % (GQ * SLOTS)
    target = (me + offset * MIX) % n
    slot_col = (which // SLOTS) * (SLOTS * n) + target * SLOTS + which % SLOTS
    pick = (slot_col == slot_wide).astype(jnp.float32).astype(jnp.bfloat16)

    load_q.wait()
    for j in range(GQ):
        for k in range(KVH):
            piece = q_v[:, (k * GQ + j) * HD : (k * GQ + j + 1) * HD]
            qp[j * rows : (j + 1) * rows, k * HD : (k + 1) * HD] = piece
    qf[...] = qp[...].astype(jnp.float32)
    send[...] = dot(pick, qp[...]).astype(jnp.bfloat16).reshape(send.shape)

    pl.semaphore_wait(barrier, n - 1)
    pltpu.make_async_copy(send.at[0], recv.at[0], recv_sem.at[0]).start()

    def send_out(i, c):
        pltpu.make_async_remote_copy(
            src_ref=send.at[i],
            dst_ref=recv.at[i],
            send_sem=send_sem,
            recv_sem=recv_sem.at[i // per],
            device_id=(lax.rem(me + i * MIX, n),),
            device_id_type=MESH,
        ).start()
        return c

    lax.fori_loop(1, n, send_out, 0)

    load_pk.wait()
    load_pv.wait()
    for k in range(KVH):
        first, end = window(k)
        wide = (end - first) * LANES
        lane = iota((1, wide), 1) + first * LANES
        keep = of_head(lane, k).astype(jnp.float32).astype(jnp.bfloat16)
        kpad[k, :, :wide] = pk_v[:, first * LANES : end * LANES] * keep
        vpad[k, :, :wide] = pv_v[:, first * LANES : end * LANES] * keep

    load_poolk.wait()
    load_poolv.wait()
    lane8 = iota((KVH, KW), 1)
    block = of_head(lane8, iota((KVH, KW), 0))
    token = iota((H, LANES), 1)
    lane_row = iota((BATCH, LANES), 1)

    def private_batch(b, c):
        for u in range(BATCH):
            r = b * BATCH + u
            parts = []
            for j in range(GQ):
                line = qf[pl.ds(j * rows + r, 1), :]
                parts.append(jnp.where(block, line, 0.0))
            query = jnp.concatenate(parts, axis=0).astype(jnp.bfloat16)
            keys = jnp.concatenate([poolk[table[p, r]] for p in range(8)], axis=0)
            values = jnp.concatenate([poolv[table[p, r]] for p in range(8)], axis=0)
            scores = dot(query, keys, NT)
            scores = jnp.where(token < lengths[r], scores, -1e30)
            largest = jnp.max(scores, axis=1, keepdims=True)
            weights = jnp.exp2((scores - largest) * (SCALE * LOG2E))
            total = jnp.sum(weights, axis=1, keepdims=True)
            summed = dot(weights.astype(jnp.bfloat16), values)
            summed = summed * (1.0 / total)
            for t in range(TILES):
                base = (t * BATCH + u) * H
                stage[base : base + H, :] = summed[:, t * LANES : (t + 1) * LANES]
            stat[u * H : (u + 1) * H, :] = jnp.broadcast_to(
                largest * SCALE + jnp.log(total), (H, LANES)
            )
        start = pl.multiple_of(b * BATCH, BATCH)
        for j in range(GQ):
            for t in range(TILES):
                lane = lane_row + t * LANES
                out = jnp.zeros((BATCH, LANES), jnp.float32)
                lse = jnp.zeros((BATCH, LANES), jnp.float32)
                for k in range(KVH):
                    first, end = window(k)
                    if first <= t < end:
                        inside = of_head(lane, k)
                        spot = pl.ds(j * KVH + k, BATCH, stride=H)
                        here = pl.ds(t * BATCH * H + j * KVH + k, BATCH, stride=H)
                        out = jnp.where(inside, stage[here, :], out)
                        lse = jnp.where(inside, stat[spot, :], lse)
                own[pl.ds(j * rows + start, BATCH), t * LANES : (t + 1) * LANES] = out
                own_lse[pl.ds(j * rows + start, BATCH), t * LANES : (t + 1) * LANES] = lse
        return c

    message = GQ * SLOTS
    span = per * message
    lane_m = iota((span, LANES), 1)

    def shared(c):
        query = recv[pl.ds(c * per, per)].reshape(span, KW)
        tiles = [None] * TILES
        lse = jnp.zeros((span, LANES), jnp.float32)
        for k in range(KVH):
            first, end = window(k)
            wide = (end - first) * LANES
            scores = dot(query[:, first * LANES : end * LANES], kpad[k, :, :wide], NT)
            largest = jnp.max(scores, axis=1, keepdims=True)
            weights = jnp.exp2((scores - largest) * (SCALE * LOG2E))
            total = jnp.sum(weights, axis=1, keepdims=True)
            summed = dot(weights.astype(jnp.bfloat16), vpad[k, :, :wide]) * (1.0 / total)
            lse = jnp.where(lane_m % KVH == k, largest * SCALE + jnp.log(total), lse)
            for t in range(first, end):
                piece = summed[:, (t - first) * LANES : (t - first + 1) * LANES]
                tiles[t] = piece if tiles[t] is None else tiles[t] + piece
        for t in range(TILES):
            result[pl.ds(c * per, per), :, t * LANES : (t + 1) * LANES] = (
                tiles[t].astype(jnp.bfloat16).reshape(per, message, LANES)
            )
        high = lse.astype(jnp.bfloat16).astype(jnp.float32)
        rest = lse - high
        middle = rest.astype(jnp.bfloat16).astype(jnp.float32)
        low = rest - middle
        three = jnp.where(lane_m < KVH, high, jnp.where(lane_m < 2 * KVH, middle, low))
        result[pl.ds(c * per, per), :, KW:] = (
            three.astype(jnp.bfloat16).reshape(per, message, LANES)
        )

    def answer(i, c):
        pltpu.make_async_remote_copy(
            src_ref=result.at[i],
            dst_ref=back.at[i],
            send_sem=back_send_sem,
            recv_sem=back_sem,
            device_id=(lax.rem(me + i * (n - MIX), n),),
            device_id_type=MESH,
        ).start()
        return c

    batches = rows // BATCH // CHUNKS

    def chunk(c, carry):
        lax.fori_loop(c * batches, (c + 1) * batches, private_batch, 0)
        arrived = recv.at[pl.ds(c * per, per)]
        pltpu.make_async_copy(arrived, arrived, recv_sem.at[c]).wait()
        shared(c)
        lax.fori_loop(jnp.maximum(c * per, 1), (c + 1) * per, answer, 0)
        return carry

    lax.fori_loop(0, CHUNKS, chunk, 0)
    pltpu.make_async_copy(result.at[0], back.at[0], back_sem).start()

    others = send.at[pl.ds(1, n - 1)]
    pltpu.make_async_copy(others, others, send_sem).wait()
    others = result.at[pl.ds(1, n - 1)]
    pltpu.make_async_copy(others, others, back_send_sem).wait()
    pltpu.make_async_copy(w_v, w_v, load_sem.at[5]).wait()
    pltpu.make_async_copy(back, back, back_sem).wait()

    returned = back[...].reshape(n * message, KW + LANES)
    spread = lax.dot_general(
        pick, returned, (((0,), (0,)), ((), ())), preferred_element_type=jnp.float32
    )
    entry = iota((LANES, KW), 0)
    expand = (entry < 3 * KVH) & of_head(iota((LANES, KW), 1), entry % KVH)
    expand = expand.astype(jnp.float32).astype(jnp.bfloat16)
    prefix_lse = dot(spread[:, KW:].astype(jnp.bfloat16), expand)
    prefix_out = spread[:, :KW]
    private_lse = own_lse[...]
    most = jnp.maximum(prefix_lse, private_lse)
    a = jnp.exp(prefix_lse - most)
    b = jnp.exp(private_lse - most)
    attended = ((a * prefix_out + b * own[...]) / (a + b)).astype(jnp.bfloat16)
    flat = jnp.concatenate([attended[j * rows : (j + 1) * rows] for j in range(GQ)], axis=1)
    width = 512
    is_live = iota((rows, width), 0) < live[0]

    for t in range(o_ref.shape[1] // width):
        projected = dot(flat, w_v[:, t * width : (t + 1) * width])
        o_ref[:, t * width : (t + 1) * width] = jnp.where(is_live, projected, 0.0).astype(
            jnp.bfloat16
        )


def per_device(
    queries,
    prefix_keys,
    prefix_values,
    pool_keys,
    pool_values,
    page_table,
    private_length,
    group_ids,
    live_rows,
    out_weight,
):
    n = lax.axis_size("req")
    rows, width = queries.shape
    tokens = prefix_keys.shape[0]
    message = GQ * SLOTS
    bf16, f32 = jnp.bfloat16, jnp.float32
    smem = pl.BlockSpec(memory_space=pltpu.SMEM)
    vmem = pl.BlockSpec(memory_space=pltpu.VMEM)
    far = pl.BlockSpec(memory_space=pl.ANY)
    return pl.pallas_call(
        functools.partial(kernel, n, rows),
        out_shape=jax.ShapeDtypeStruct((rows, width), bf16),
        in_specs=[smem, smem, smem, vmem] + [far] * 6,
        out_specs=vmem,
        scratch_shapes=[
            pltpu.VMEM(queries.shape, bf16),
            pltpu.VMEM(prefix_keys.shape, bf16),
            pltpu.VMEM(prefix_values.shape, bf16),
            pltpu.VMEM(pool_keys.shape, bf16),
            pltpu.VMEM(pool_values.shape, bf16),
            pltpu.VMEM(out_weight.shape, bf16),
            pltpu.VMEM((GQ * rows, KW), bf16),
            pltpu.VMEM((GQ * rows, KW), f32),
            pltpu.VMEM((KVH, tokens, 2 * LANES), bf16),
            pltpu.VMEM((KVH, tokens, 2 * LANES), bf16),
            pltpu.VMEM((n, message, KW), bf16),
            pltpu.VMEM((n, message, KW), bf16),
            pltpu.VMEM((n, message, KW + LANES), bf16),
            pltpu.VMEM((n, message, KW + LANES), bf16),
            pltpu.VMEM((TILES * BATCH * H, LANES), f32),
            pltpu.VMEM((BATCH * H, LANES), f32),
            pltpu.VMEM((GQ * rows, KW), f32),
            pltpu.VMEM((GQ * rows, KW), f32),
            pltpu.SemaphoreType.DMA((6,)),
            pltpu.SemaphoreType.DMA,
            pltpu.SemaphoreType.DMA((CHUNKS,)),
            pltpu.SemaphoreType.DMA,
            pltpu.SemaphoreType.DMA,
        ],
        compiler_params=pltpu.CompilerParams(
            collective_id=0, has_side_effects=True, vmem_limit_bytes=60 << 20
        ),
    )(
        page_table.T,
        private_length,
        live_rows,
        group_ids.reshape(1, rows),
        queries,
        prefix_keys,
        prefix_values,
        pool_keys,
        pool_values,
        out_weight,
    )


def solution(mesh):
    placed = (
        P("req", None),
        P("req", None),
        P("req", None),
        P("req", None, None),
        P("req", None, None),
        P("req", None),
        P("req"),
        P("req", None),
        P("req"),
        P(),
    )
    return jax.shard_map(
        per_device, mesh=mesh, in_specs=placed, out_specs=P("req", None), check_vma=False
    )
```

```python
import functools

import jax
import jax.numpy as jnp
from jax import lax
from jax.experimental import pallas as pl
from jax.experimental.pallas import tpu as pltpu
from jax.sharding import PartitionSpec as P

MESH = pl.DeviceIdType.MESH
H = 32
KVH = 8
HD = 80
GQ = H // KVH
KW = KVH * HD
LANES = 128
TILES = KW // LANES
SLOTS = 2
MIX = 45
CHUNKS = 4
BATCH = 8
SCALE = HD ** (-0.5)
LOG2E = 1.4426950408889634
NT = (((1,), (1,)), ((), ()))
NN = (((1,), (0,)), ((), ()))


def dot(a, b, dims=NN):
    return lax.dot_general(a, b, dims, preferred_element_type=jnp.float32)


def iota(shape, axis):
    return lax.broadcasted_iota(jnp.int32, shape, axis)


def window(k):
    first = k * HD // LANES
    last = (k * HD + HD - 1) // LANES
    return first, last + 1


def of_head(lane, k):
    return (lane >= k * HD) & (lane < (k + 1) * HD)


def kernel(
    n,
    rows,
    table,
    lengths,
    live,
    groups,
    q_hbm,
    pk_hbm,
    pv_hbm,
    poolk_hbm,
    poolv_hbm,
    w_hbm,
    o_ref,
    q_v,
    pk_v,
    pv_v,
    poolk,
    poolv,
    w_v,
    qp,
    qf,
    kpad,
    vpad,
    send,
    recv,
    result,
    back,
    stage,
    stat,
    own,
    own_lse,
    load_sem,
    send_sem,
    recv_sem,
    back_send_sem,
    back_sem,
):
    me = lax.axis_index("req")
    per = n // CHUNKS
    load_q = pltpu.make_async_copy(q_hbm, q_v, load_sem.at[0])
    load_pk = pltpu.make_async_copy(pk_hbm, pk_v, load_sem.at[1])
    load_pv = pltpu.make_async_copy(pv_hbm, pv_v, load_sem.at[2])
    load_poolk = pltpu.make_async_copy(poolk_hbm, poolk, load_sem.at[3])
    load_poolv = pltpu.make_async_copy(poolv_hbm, poolv, load_sem.at[4])
    load_q.start()
    barrier = pltpu.get_barrier_semaphore()

    def greet(i, c):
        pl.semaphore_signal(
            barrier, inc=1, device_id=(lax.rem(me + i, n),), device_id_type=MESH
        )
        return c

    lax.fori_loop(1, n, greet, 0)
    load_pk.start()
    load_pv.start()
    load_poolk.start()
    load_poolv.start()

    def load_w(b, c):
        source = (lax.rem(b, KVH) * GQ + b // KVH) * HD
        pltpu.make_async_copy(
            w_hbm.at[pl.ds(pl.multiple_of(source, 16), HD)],
            w_v.at[pl.ds(pl.multiple_of(b * HD, 16), HD)],
            load_sem.at[5],
        ).start()
        return c

    lax.fori_loop(0, H, load_w, 0)

    group_row = groups[...]
    eye = iota((rows, rows), 0) == iota((rows, rows), 1)
    group_col = jnp.sum(jnp.where(eye, group_row, 0), axis=1, keepdims=True)
    earlier = (group_col == group_row) & (iota((rows, rows), 0) < iota((rows, rows), 1))
    rank = jnp.sum(earlier.astype(jnp.int32), axis=0, keepdims=True)
    slot_row = group_row * SLOTS + rank
    slot_wide = jnp.concatenate([slot_row + j * (SLOTS * n) for j in range(GQ)], axis=1)
    index = iota((n * GQ * SLOTS, 1), 0)
    offset = index // (GQ * SLOTS)
    which = index % (GQ * SLOTS)
    target = (me + offset * MIX) % n
    slot_col = (which // SLOTS) * (SLOTS * n) + target * SLOTS + which % SLOTS
    pick = (slot_col == slot_wide).astype(jnp.float32).astype(jnp.bfloat16)

    load_q.wait()
    for j in range(GQ):
        for k in range(KVH):
            piece = q_v[:, (k * GQ + j) * HD : (k * GQ + j + 1) * HD]
            qp[j * rows : (j + 1) * rows, k * HD : (k + 1) * HD] = piece
    qf[...] = qp[...].astype(jnp.float32)
    send[...] = dot(pick, qp[...]).astype(jnp.bfloat16).reshape(send.shape)

    pl.semaphore_wait(barrier, n - 1)
    pltpu.make_async_copy(send.at[0], recv.at[0], recv_sem.at[0]).start()

    def send_out(i, c):
        pltpu.make_async_remote_copy(
            src_ref=send.at[i],
            dst_ref=recv.at[i],
            send_sem=send_sem,
            recv_sem=recv_sem.at[i // per],
            device_id=(lax.rem(me + i * MIX, n),),
            device_id_type=MESH,
        ).start()
        return c

    lax.fori_loop(1, n, send_out, 0)

    load_pk.wait()
    load_pv.wait()
    for k in range(KVH):
        first, end = window(k)
        wide = (end - first) * LANES
        lane = iota((1, wide), 1) + first * LANES
        keep = of_head(lane, k).astype(jnp.float32).astype(jnp.bfloat16)
        kpad[k, :, :wide] = pk_v[:, first * LANES : end * LANES] * keep
        vpad[k, :, :wide] = pv_v[:, first * LANES : end * LANES] * keep

    load_poolk.wait()
    load_poolv.wait()
    lane8 = iota((KVH, KW), 1)
    block = of_head(lane8, iota((KVH, KW), 0))
    token = iota((H, LANES), 1)
    lane_row = iota((BATCH, LANES), 1)

    def private_batch(b, c):
        all_scores = []
        for u in range(BATCH):
            r = b * BATCH + u
            parts = []
            for j in range(GQ):
                line = qf[pl.ds(j * rows + r, 1), :]
                parts.append(jnp.where(block, line, 0.0))
            query = jnp.concatenate(parts, axis=0).astype(jnp.bfloat16)
            keys = jnp.concatenate([poolk[table[p, r]] for p in range(8)], axis=0)
            scores = dot(query, keys, NT)
            all_scores.append(jnp.where(token < lengths[r], scores, -1e30))
        scores = jnp.concatenate(all_scores, axis=0)
        largest = jnp.max(scores, axis=1, keepdims=True)
        weights = jnp.exp2((scores - largest) * (SCALE * LOG2E))
        total = jnp.sum(weights, axis=1, keepdims=True)
        share = 1.0 / total
        rounded = weights.astype(jnp.bfloat16)
        stat[...] = jnp.broadcast_to(largest * SCALE + jnp.log(total), stat.shape)
        for u in range(BATCH):
            r = b * BATCH + u
            values = jnp.concatenate([poolv[table[p, r]] for p in range(8)], axis=0)
            summed = dot(rounded[u * H : (u + 1) * H], values)
            summed = summed * share[u * H : (u + 1) * H]
            for t in range(TILES):
                base = (t * BATCH + u) * H
                stage[base : base + H, :] = summed[:, t * LANES : (t + 1) * LANES]
        start = pl.multiple_of(b * BATCH, BATCH)
        for j in range(GQ):
            for t in range(TILES):
                lane = lane_row + t * LANES
                out = jnp.zeros((BATCH, LANES), jnp.float32)
                lse = jnp.zeros((BATCH, LANES), jnp.float32)
                for k in range(KVH):
                    first, end = window(k)
                    if first <= t < end:
                        inside = of_head(lane, k)
                        spot = pl.ds(j * KVH + k, BATCH, stride=H)
                        here = pl.ds(t * BATCH * H + j * KVH + k, BATCH, stride=H)
                        out = jnp.where(inside, stage[here, :], out)
                        lse = jnp.where(inside, stat[spot, :], lse)
                own[pl.ds(j * rows + start, BATCH), t * LANES : (t + 1) * LANES] = out
                own_lse[pl.ds(j * rows + start, BATCH), t * LANES : (t + 1) * LANES] = lse
        return c

    message = GQ * SLOTS
    span = per * message
    lane_m = iota((span, LANES), 1)

    def shared(c):
        query = recv[pl.ds(c * per, per)].reshape(span, KW)
        tiles = [None] * TILES
        lse = jnp.zeros((span, LANES), jnp.float32)
        for k in range(KVH):
            first, end = window(k)
            wide = (end - first) * LANES
            scores = dot(query[:, first * LANES : end * LANES], kpad[k, :, :wide], NT)
            largest = jnp.max(scores, axis=1, keepdims=True)
            weights = jnp.exp2((scores - largest) * (SCALE * LOG2E))
            total = jnp.sum(weights, axis=1, keepdims=True)
            summed = dot(weights.astype(jnp.bfloat16), vpad[k, :, :wide]) * (1.0 / total)
            lse = jnp.where(lane_m % KVH == k, largest * SCALE + jnp.log(total), lse)
            for t in range(first, end):
                piece = summed[:, (t - first) * LANES : (t - first + 1) * LANES]
                tiles[t] = piece if tiles[t] is None else tiles[t] + piece
        for t in range(TILES):
            result[pl.ds(c * per, per), :, t * LANES : (t + 1) * LANES] = (
                tiles[t].astype(jnp.bfloat16).reshape(per, message, LANES)
            )
        high = lse.astype(jnp.bfloat16).astype(jnp.float32)
        rest = lse - high
        middle = rest.astype(jnp.bfloat16).astype(jnp.float32)
        low = rest - middle
        three = jnp.where(lane_m < KVH, high, jnp.where(lane_m < 2 * KVH, middle, low))
        result[pl.ds(c * per, per), :, KW:] = (
            three.astype(jnp.bfloat16).reshape(per, message, LANES)
        )

    def answer(i, c):
        pltpu.make_async_remote_copy(
            src_ref=result.at[i],
            dst_ref=back.at[i],
            send_sem=back_send_sem,
            recv_sem=back_sem,
            device_id=(lax.rem(me + i * (n - MIX), n),),
            device_id_type=MESH,
        ).start()
        return c

    batches = rows // BATCH // CHUNKS

    def chunk(c, carry):
        lax.fori_loop(c * batches, (c + 1) * batches, private_batch, 0)
        arrived = recv.at[pl.ds(c * per, per)]
        pltpu.make_async_copy(arrived, arrived, recv_sem.at[c]).wait()
        shared(c)
        lax.fori_loop(jnp.maximum(c * per, 1), (c + 1) * per, answer, 0)
        return carry

    lax.fori_loop(0, CHUNKS, chunk, 0)
    pltpu.make_async_copy(result.at[0], back.at[0], back_sem).start()

    others = send.at[pl.ds(1, n - 1)]
    pltpu.make_async_copy(others, others, send_sem).wait()
    others = result.at[pl.ds(1, n - 1)]
    pltpu.make_async_copy(others, others, back_send_sem).wait()
    pltpu.make_async_copy(w_v, w_v, load_sem.at[5]).wait()
    pltpu.make_async_copy(back, back, back_sem).wait()

    returned = back[...].reshape(n * message, KW + LANES)
    spread = lax.dot_general(
        pick, returned, (((0,), (0,)), ((), ())), preferred_element_type=jnp.float32
    )
    entry = iota((LANES, KW), 0)
    expand = (entry < 3 * KVH) & of_head(iota((LANES, KW), 1), entry % KVH)
    expand = expand.astype(jnp.float32).astype(jnp.bfloat16)
    prefix_lse = dot(spread[:, KW:].astype(jnp.bfloat16), expand)
    prefix_out = spread[:, :KW]
    private_lse = own_lse[...]
    most = jnp.maximum(prefix_lse, private_lse)
    a = jnp.exp(prefix_lse - most)
    b = jnp.exp(private_lse - most)
    attended = ((a * prefix_out + b * own[...]) / (a + b)).astype(jnp.bfloat16)
    flat = jnp.concatenate([attended[j * rows : (j + 1) * rows] for j in range(GQ)], axis=1)
    width = 512
    is_live = iota((rows, width), 0) < live[0]

    for t in range(o_ref.shape[1] // width):
        projected = dot(flat, w_v[:, t * width : (t + 1) * width])
        o_ref[:, t * width : (t + 1) * width] = jnp.where(is_live, projected, 0.0).astype(
            jnp.bfloat16
        )


def per_device(
    queries,
    prefix_keys,
    prefix_values,
    pool_keys,
    pool_values,
    page_table,
    private_length,
    group_ids,
    live_rows,
    out_weight,
):
    n = lax.axis_size("req")
    rows, width = queries.shape
    tokens = prefix_keys.shape[0]
    message = GQ * SLOTS
    bf16, f32 = jnp.bfloat16, jnp.float32
    smem = pl.BlockSpec(memory_space=pltpu.SMEM)
    vmem = pl.BlockSpec(memory_space=pltpu.VMEM)
    far = pl.BlockSpec(memory_space=pl.ANY)
    return pl.pallas_call(
        functools.partial(kernel, n, rows),
        out_shape=jax.ShapeDtypeStruct((rows, width), bf16),
        in_specs=[smem, smem, smem, vmem] + [far] * 6,
        out_specs=vmem,
        scratch_shapes=[
            pltpu.VMEM(queries.shape, bf16),
            pltpu.VMEM(prefix_keys.shape, bf16),
            pltpu.VMEM(prefix_values.shape, bf16),
            pltpu.VMEM(pool_keys.shape, bf16),
            pltpu.VMEM(pool_values.shape, bf16),
            pltpu.VMEM(out_weight.shape, bf16),
            pltpu.VMEM((GQ * rows, KW), bf16),
            pltpu.VMEM((GQ * rows, KW), f32),
            pltpu.VMEM((KVH, tokens, 2 * LANES), bf16),
            pltpu.VMEM((KVH, tokens, 2 * LANES), bf16),
            pltpu.VMEM((n, message, KW), bf16),
            pltpu.VMEM((n, message, KW), bf16),
            pltpu.VMEM((n, message, KW + LANES), bf16),
            pltpu.VMEM((n, message, KW + LANES), bf16),
            pltpu.VMEM((TILES * BATCH * H, LANES), f32),
            pltpu.VMEM((BATCH * H, LANES), f32),
            pltpu.VMEM((GQ * rows, KW), f32),
            pltpu.VMEM((GQ * rows, KW), f32),
            pltpu.SemaphoreType.DMA((6,)),
            pltpu.SemaphoreType.DMA,
            pltpu.SemaphoreType.DMA((CHUNKS,)),
            pltpu.SemaphoreType.DMA,
            pltpu.SemaphoreType.DMA,
        ],
        compiler_params=pltpu.CompilerParams(
            collective_id=0, has_side_effects=True, vmem_limit_bytes=60 << 20
        ),
    )(
        page_table.T,
        private_length,
        live_rows,
        group_ids.reshape(1, rows),
        queries,
        prefix_keys,
        prefix_values,
        pool_keys,
        pool_values,
        out_weight,
    )


def solution(mesh):
    placed = (
        P("req", None),
        P("req", None),
        P("req", None),
        P("req", None, None),
        P("req", None, None),
        P("req", None),
        P("req"),
        P("req", None),
        P("req"),
        P(),
    )
    return jax.shard_map(
        per_device, mesh=mesh, in_specs=placed, out_specs=P("req", None), check_vma=False
    )
```

```python
import functools

import jax
import jax.numpy as jnp
from jax import lax
from jax.experimental import pallas as pl
from jax.experimental.pallas import tpu as pltpu
from jax.sharding import PartitionSpec as P

MESH = pl.DeviceIdType.MESH
H = 32
KVH = 8
HD = 80
GQ = H // KVH
KW = KVH * HD
LANES = 128
TILES = KW // LANES
SLOTS = 2
MIX = 45
CHUNKS = 4
BATCH = 8
EARLY = 3
EACH = 2
SCALE = HD ** (-0.5)
LOG2E = 1.4426950408889634
NT = (((1,), (1,)), ((), ()))
NN = (((1,), (0,)), ((), ()))


def dot(a, b, dims=NN):
    return lax.dot_general(a, b, dims, preferred_element_type=jnp.float32)


def iota(shape, axis):
    return lax.broadcasted_iota(jnp.int32, shape, axis)


def window(k):
    first = k * HD // LANES
    last = (k * HD + HD - 1) // LANES
    return first, last + 1


def of_head(lane, k):
    return (lane >= k * HD) & (lane < (k + 1) * HD)


def kernel(
    n,
    rows,
    table_hbm,
    lengths_hbm,
    groups_hbm,
    q_hbm,
    pk_hbm,
    pv_hbm,
    poolk_hbm,
    poolv_hbm,
    w_hbm,
    o_ref,
    table,
    lengths,
    groups,
    q_v,
    pk_v,
    pv_v,
    poolk,
    poolv,
    w_v,
    qp,
    qf,
    kpad,
    vpad,
    send,
    recv,
    result,
    back,
    lse_out,
    lse_back,
    stage,
    stat,
    own,
    own_lse,
    pick,
    spread,
    load_sem,
    send_sem,
    recv_sem,
    back_send_sem,
    back_sem,
    lse_send_sem,
    lse_sem,
):
    me = lax.axis_index("req")
    per = n // CHUNKS
    load_q = pltpu.make_async_copy(q_hbm, q_v, load_sem.at[0])
    load_pk = pltpu.make_async_copy(pk_hbm, pk_v, load_sem.at[1])
    load_pv = pltpu.make_async_copy(pv_hbm, pv_v, load_sem.at[2])
    load_poolk = pltpu.make_async_copy(poolk_hbm, poolk, load_sem.at[3])
    load_poolv = pltpu.make_async_copy(poolv_hbm, poolv, load_sem.at[4])
    load_table = pltpu.make_async_copy(table_hbm, table, load_sem.at[6])
    load_lengths = pltpu.make_async_copy(lengths_hbm, lengths, load_sem.at[7])
    load_groups = pltpu.make_async_copy(groups_hbm, groups, load_sem.at[8])
    load_groups.start()
    load_q.start()
    load_table.start()
    load_lengths.start()
    barrier = pltpu.get_barrier_semaphore()

    def greet(i, c):
        pl.semaphore_signal(
            barrier, inc=1, device_id=(lax.rem(me + i, n),), device_id_type=MESH
        )
        return c

    lax.fori_loop(1, n, greet, 0, unroll=8)
    load_pk.start()
    load_pv.start()
    load_poolk.start()
    load_poolv.start()

    def load_w(b, c):
        source = (lax.rem(b, KVH) * GQ + b // KVH) * HD
        pltpu.make_async_copy(
            w_hbm.at[pl.ds(pl.multiple_of(source, 16), HD)],
            w_v.at[pl.ds(pl.multiple_of(b * HD, 16), HD)],
            load_sem.at[5],
        ).start()
        return c

    lax.fori_loop(0, H, load_w, 0)

    load_groups.wait()
    group_row = groups[...]
    eye = iota((rows, rows), 0) == iota((rows, rows), 1)
    group_col = jnp.sum(jnp.where(eye, group_row, 0), axis=1, keepdims=True)
    earlier = (group_col == group_row) & (iota((rows, rows), 0) < iota((rows, rows), 1))
    rank = jnp.sum(earlier.astype(jnp.int32), axis=0, keepdims=True)
    slot_row = group_row * SLOTS + rank
    slot_wide = jnp.concatenate([slot_row + j * (SLOTS * n) for j in range(GQ)], axis=1)
    index = iota((n * GQ * SLOTS, 1), 0)
    offset = index // (GQ * SLOTS)
    which = index % (GQ * SLOTS)
    target = (me + offset * MIX) % n
    slot_col = (which // SLOTS) * (SLOTS * n) + target * SLOTS + which % SLOTS
    pick[...] = (slot_col == slot_wide).astype(jnp.float32).astype(jnp.bfloat16)
    rank_col = jnp.sum(jnp.where(eye, rank, 0), axis=1, keepdims=True)

    load_q.wait()
    for j in range(GQ):
        for k in range(KVH):
            piece = q_v[:, (k * GQ + j) * HD : (k * GQ + j + 1) * HD]
            qp[j * rows : (j + 1) * rows, k * HD : (k + 1) * HD] = piece
    qf[...] = qp[...].astype(jnp.float32)
    send[...] = dot(pick[...], qp[...]).astype(jnp.bfloat16).reshape(send.shape)

    pl.semaphore_wait(barrier, n - 1)
    pltpu.make_async_copy(send.at[0], recv.at[0], recv_sem.at[0]).start()

    def send_out(i, c):
        pltpu.make_async_remote_copy(
            src_ref=send.at[i],
            dst_ref=recv.at[i],
            send_sem=send_sem,
            recv_sem=recv_sem.at[i // per],
            device_id=(lax.rem(me + i * MIX, n),),
            device_id_type=MESH,
        ).start()
        return c

    lax.fori_loop(1, n, send_out, 0)

    load_pk.wait()
    load_pv.wait()
    for k in range(KVH):
        first, end = window(k)
        wide = (end - first) * LANES
        lane = iota((1, wide), 1) + first * LANES
        keep = of_head(lane, k).astype(jnp.float32).astype(jnp.bfloat16)
        kpad[k, :, :wide] = pk_v[:, first * LANES : end * LANES] * keep
        vpad[k, :, :wide] = pv_v[:, first * LANES : end * LANES] * keep

    load_table.wait()
    load_lengths.wait()
    load_poolk.wait()
    load_poolv.wait()
    lane8 = iota((KVH, KW), 1)
    block = of_head(lane8, iota((KVH, KW), 0))
    token = iota((H, LANES), 1)
    lane_row = iota((BATCH, LANES), 1)

    def private_batch(b, c):
        all_scores = []
        for u in range(BATCH):
            r = b * BATCH + u
            parts = []
            for j in range(GQ):
                line = qf[pl.ds(j * rows + r, 1), :]
                parts.append(jnp.where(block, line, 0.0))
            query = jnp.concatenate(parts, axis=0).astype(jnp.bfloat16)
            keys = jnp.concatenate([poolk[table[p, r]] for p in range(8)], axis=0)
            scores = dot(query, keys, NT)
            all_scores.append(jnp.where(token < lengths[r], scores, -1e30))
        scores = jnp.concatenate(all_scores, axis=0)
        largest = jnp.max(scores, axis=1, keepdims=True)
        weights = jnp.exp2((scores - largest) * (SCALE * LOG2E))
        total = jnp.sum(weights, axis=1, keepdims=True)
        share = 1.0 / total
        rounded = weights.astype(jnp.bfloat16)
        stat[...] = jnp.broadcast_to(largest * SCALE + jnp.log(total), stat.shape)
        for u in range(BATCH):
            r = b * BATCH + u
            values = jnp.concatenate([poolv[table[p, r]] for p in range(8)], axis=0)
            summed = dot(rounded[u * H : (u + 1) * H], values)
            summed = summed * share[u * H : (u + 1) * H]
            for t in range(TILES):
                base = (t * BATCH + u) * H
                stage[base : base + H, :] = summed[:, t * LANES : (t + 1) * LANES]
        start = pl.multiple_of(b * BATCH, BATCH)
        for j in range(GQ):
            for t in range(TILES):
                lane = lane_row + t * LANES
                out = jnp.zeros((BATCH, LANES), jnp.float32)
                lse = jnp.zeros((BATCH, LANES), jnp.float32)
                for k in range(KVH):
                    first, end = window(k)
                    if first <= t < end:
                        inside = of_head(lane, k)
                        spot = pl.ds(j * KVH + k, BATCH, stride=H)
                        here = pl.ds(t * BATCH * H + j * KVH + k, BATCH, stride=H)
                        out = jnp.where(inside, stage[here, :], out)
                        lse = jnp.where(inside, stat[spot, :], lse)
                own[pl.ds(j * rows + start, BATCH), t * LANES : (t + 1) * LANES] = out
                own_lse[pl.ds(j * rows + start, BATCH), t * LANES : (t + 1) * LANES] = lse
        return c

    message = GQ * SLOTS
    span = per * message
    lane_m = iota((span, LANES), 1)

    def shared(c):
        query = recv[pl.ds(c * per, per)].reshape(span, KW)
        tiles = [None] * TILES
        lse = jnp.zeros((span, LANES), jnp.float32)
        for k in range(KVH):
            first, end = window(k)
            wide = (end - first) * LANES
            scores = dot(query[:, first * LANES : end * LANES], kpad[k, :, :wide], NT)
            largest = jnp.max(scores, axis=1, keepdims=True)
            weights = jnp.exp2((scores - largest) * (SCALE * LOG2E))
            total = jnp.sum(weights, axis=1, keepdims=True)
            summed = dot(weights.astype(jnp.bfloat16), vpad[k, :, :wide]) * (1.0 / total)
            lse = jnp.where(lane_m % KVH == k, largest * SCALE + jnp.log(total), lse)
            for t in range(first, end):
                piece = summed[:, (t - first) * LANES : (t - first + 1) * LANES]
                tiles[t] = piece if tiles[t] is None else tiles[t] + piece
        for t in range(TILES):
            result[pl.ds(c * per, per), :, t * LANES : (t + 1) * LANES] = (
                tiles[t].astype(jnp.bfloat16).reshape(per, message, LANES)
            )
        line = iota((span, LANES), 0) % message
        lse = jnp.where(lane_m // KVH == line, lse, 0.0)
        lse_out[pl.ds(c * per, per)] = jnp.sum(
            lse.reshape(per, message, LANES), axis=1, keepdims=True
        )

    def answer(i, c):
        pltpu.make_async_remote_copy(
            src_ref=result.at[i],
            dst_ref=back.at[i],
            send_sem=back_send_sem,
            recv_sem=back_sem.at[i // per],
            device_id=(lax.rem(me + i * (n - MIX), n),),
            device_id_type=MESH,
        ).start()
        pltpu.make_async_remote_copy(
            src_ref=lse_out.at[i],
            dst_ref=lse_back.at[i],
            send_sem=lse_send_sem,
            recv_sem=lse_sem,
            device_id=(lax.rem(me + i * (n - MIX), n),),
            device_id_type=MESH,
        ).start()
        return c

    def chunk(c, carry):
        until = EARLY + EACH * c
        lax.fori_loop(jnp.where(c == 0, 0, until - EACH), until, private_batch, 0)
        arrived = recv.at[pl.ds(c * per, per)]
        pltpu.make_async_copy(arrived, arrived, recv_sem.at[c]).wait()
        shared(c)
        lax.fori_loop(jnp.maximum(c * per, 1), (c + 1) * per, answer, 0)
        return carry

    lax.fori_loop(0, CHUNKS, chunk, 0)
    pltpu.make_async_copy(result.at[0], back.at[0], back_sem.at[0]).start()
    pltpu.make_async_copy(lse_out.at[0], lse_back.at[0], lse_sem).start()
    lax.fori_loop(EARLY + EACH * (CHUNKS - 1), rows // BATCH, private_batch, 0)

    others = send.at[pl.ds(1, n - 1)]
    pltpu.make_async_copy(others, others, send_sem).wait()
    pltpu.make_async_copy(w_v, w_v, load_sem.at[5]).wait()

    spread[...] = jnp.zeros(spread.shape, jnp.float32)

    def gather(c, carry):
        returned = back.at[pl.ds(c * per, per)]
        pltpu.make_async_copy(returned, returned, back_sem.at[c]).wait()
        spread[...] += lax.dot_general(
            pick[pl.ds(c * span, span), :],
            back[pl.ds(c * per, per)].reshape(span, KW),
            (((0,), (0,)), ((), ())),
            preferred_element_type=jnp.float32,
        )
        return carry

    lax.fori_loop(0, CHUNKS, gather, 0)
    others = result.at[pl.ds(1, n - 1)]
    pltpu.make_async_copy(others, others, back_send_sem).wait()
    others = lse_out.at[pl.ds(1, n - 1)]
    pltpu.make_async_copy(others, others, lse_send_sem).wait()
    pltpu.make_async_copy(lse_back, lse_back, lse_sem).wait()

    lse = lse_back[...].reshape(n, LANES)
    high = lse.astype(jnp.bfloat16)
    rest = lse - high.astype(jnp.float32)
    middle = rest.astype(jnp.bfloat16)
    low = (rest - middle.astype(jnp.float32)).astype(jnp.bfloat16)
    from_group = (group_col == (me + iota((rows, n), 1) * MIX) % n)
    from_group = from_group.astype(jnp.float32).astype(jnp.bfloat16)
    lines = dot(from_group, jnp.concatenate([high, middle, low], axis=1))
    lane3 = iota((rows, 3 * LANES), 1)
    mine = lane3 // KVH % SLOTS == rank_col
    lines = jnp.concatenate(
        [
            jnp.where(mine & (lane3 % LANES // (KVH * SLOTS) == j), lines, 0.0)
            for j in range(GQ)
        ],
        axis=0,
    )
    expand = of_head(iota((3 * LANES, KW), 1), iota((3 * LANES, KW), 0) % KVH)
    expand = expand.astype(jnp.float32).astype(jnp.bfloat16)
    prefix_lse = dot(lines.astype(jnp.bfloat16), expand)
    prefix_out = spread[...]
    private_lse = own_lse[...]
    most = jnp.maximum(prefix_lse, private_lse)
    a = jnp.exp(prefix_lse - most)
    b = jnp.exp(private_lse - most)
    attended = ((a * prefix_out + b * own[...]) / (a + b)).astype(jnp.bfloat16)
    flat = jnp.concatenate([attended[j * rows : (j + 1) * rows] for j in range(GQ)], axis=1)
    width = 512
    for t in range(o_ref.shape[1] // width):
        projected = dot(flat, w_v[:, t * width : (t + 1) * width])
        o_ref[:, t * width : (t + 1) * width] = projected.astype(jnp.bfloat16)


def per_device(
    queries,
    prefix_keys,
    prefix_values,
    pool_keys,
    pool_values,
    page_table,
    private_length,
    group_ids,
    live_rows,
    out_weight,
):
    n = lax.axis_size("req")
    rows, width = queries.shape
    tokens = prefix_keys.shape[0]
    message = GQ * SLOTS
    bf16, f32 = jnp.bfloat16, jnp.float32
    vmem = pl.BlockSpec(memory_space=pltpu.VMEM)
    far = pl.BlockSpec(memory_space=pltpu.HBM)
    projected = pl.pallas_call(
        functools.partial(kernel, n, rows),
        out_shape=jax.ShapeDtypeStruct((rows, width), bf16),
        in_specs=[far] * 9,
        out_specs=vmem,
        scratch_shapes=[
            pltpu.SMEM(page_table.shape[::-1], jnp.int32),
            pltpu.SMEM(private_length.shape, jnp.int32),
            pltpu.VMEM((1, rows), jnp.int32),
            pltpu.VMEM(queries.shape, bf16),
            pltpu.VMEM(prefix_keys.shape, bf16),
            pltpu.VMEM(prefix_values.shape, bf16),
            pltpu.VMEM(pool_keys.shape, bf16),
            pltpu.VMEM(pool_values.shape, bf16),
            pltpu.VMEM(out_weight.shape, bf16),
            pltpu.VMEM((GQ * rows, KW), bf16),
            pltpu.VMEM((GQ * rows, KW), f32),
            pltpu.VMEM((KVH, tokens, 2 * LANES), bf16),
            pltpu.VMEM((KVH, tokens, 2 * LANES), bf16),
            pltpu.VMEM((n, message, KW), bf16),
            pltpu.VMEM((n, message, KW), bf16),
            pltpu.VMEM((n, message, KW), bf16),
            pltpu.VMEM((n, message, KW), bf16),
            pltpu.VMEM((n, 1, LANES), f32),
            pltpu.VMEM((n, 1, LANES), f32),
            pltpu.VMEM((TILES * BATCH * H, LANES), f32),
            pltpu.VMEM((BATCH * H, LANES), f32),
            pltpu.VMEM((GQ * rows, KW), f32),
            pltpu.VMEM((GQ * rows, KW), f32),
            pltpu.VMEM((n * message, GQ * rows), bf16),
            pltpu.VMEM((GQ * rows, KW), f32),
            pltpu.SemaphoreType.DMA((9,)),
            pltpu.SemaphoreType.DMA,
            pltpu.SemaphoreType.DMA((CHUNKS,)),
            pltpu.SemaphoreType.DMA,
            pltpu.SemaphoreType.DMA((CHUNKS,)),
            pltpu.SemaphoreType.DMA,
            pltpu.SemaphoreType.DMA,
        ],
        compiler_params=pltpu.CompilerParams(
            collective_id=0, has_side_effects=True, vmem_limit_bytes=48 << 20
        ),
    )(
        *(
            pltpu.with_memory_space_constraint(x, pltpu.HBM)
            for x in (
                page_table.T,
                private_length,
                group_ids.reshape(1, rows),
                queries,
                prefix_keys,
                prefix_values,
                pool_keys,
                pool_values,
                out_weight,
            )
        )
    )
    is_live = jnp.arange(rows, dtype=jnp.int32)[:, None] < live_rows[0]
    return jnp.where(is_live, projected, jnp.zeros_like(projected))


def solution(mesh):
    placed = (
        P("req", None),
        P("req", None),
        P("req", None),
        P("req", None, None),
        P("req", None, None),
        P("req", None),
        P("req"),
        P("req", None),
        P("req"),
        P(),
    )
    return jax.shard_map(
        per_device, mesh=mesh, in_specs=placed, out_specs=P("req", None), check_vma=False
    )
```

```python
import functools

import jax
import jax.numpy as jnp
from jax import lax
from jax.experimental import pallas as pl
from jax.experimental.pallas import tpu as pltpu
from jax.sharding import PartitionSpec as P

MESH = pl.DeviceIdType.MESH
H = 32
KVH = 8
HD = 80
GQ = H // KVH
KW = KVH * HD
LANES = 128
TILES = KW // LANES
SLOTS = 2
MIX = 45
CHUNKS = 4
BATCH = 16
PAGES = 8
EARLY = 2
EACH = 1
SCALE = HD ** (-0.5)
LOG2E = 1.4426950408889634
NT = (((1,), (1,)), ((), ()))
NN = (((1,), (0,)), ((), ()))


def dot(a, b, dims=NN):
    return lax.dot_general(a, b, dims, preferred_element_type=jnp.float32)


def iota(shape, axis):
    return lax.broadcasted_iota(jnp.int32, shape, axis)


def window(k):
    first = k * HD // LANES
    last = (k * HD + HD - 1) // LANES
    return first, last + 1


def of_head(lane, k):
    return (lane >= k * HD) & (lane < (k + 1) * HD)


def kernel(
    n,
    rows,
    table_hbm,
    lengths_hbm,
    groups_hbm,
    q_hbm,
    pk_hbm,
    pv_hbm,
    poolk_hbm,
    poolv_hbm,
    w_hbm,
    o_ref,
    table,
    lengths,
    groups,
    q_v,
    pk_v,
    pv_v,
    poolk,
    poolv,
    w_v,
    qp,
    qf,
    kpad,
    vpad,
    send,
    recv,
    result,
    back,
    lse_out,
    lse_back,
    stage,
    stat,
    own,
    own_lse,
    pick_back,
    spread,
    load_sem,
    send_sem,
    recv_sem,
    back_send_sem,
    back_sem,
    lse_send_sem,
    lse_sem,
):
    me = lax.axis_index("req")
    per = n // CHUNKS
    load_q = pltpu.make_async_copy(q_hbm, q_v, load_sem.at[0])
    load_pk = pltpu.make_async_copy(pk_hbm, pk_v, load_sem.at[1])
    load_pv = pltpu.make_async_copy(pv_hbm, pv_v, load_sem.at[2])
    load_poolk = pltpu.make_async_copy(poolk_hbm, poolk, load_sem.at[3])
    load_poolv = pltpu.make_async_copy(poolv_hbm, poolv, load_sem.at[4])
    load_table = pltpu.make_async_copy(table_hbm, table, load_sem.at[6])
    load_lengths = pltpu.make_async_copy(lengths_hbm, lengths, load_sem.at[7])
    load_groups = pltpu.make_async_copy(groups_hbm, groups, load_sem.at[8])
    load_groups.start()
    load_q.start()
    load_table.start()
    load_lengths.start()
    barrier = pltpu.get_barrier_semaphore()

    def greet(i, c):
        pl.semaphore_signal(
            barrier, inc=1, device_id=(lax.rem(me + i, n),), device_id_type=MESH
        )
        return c

    lax.fori_loop(1, n, greet, 0, unroll=8)
    load_pk.start()
    load_pv.start()
    load_poolk.start()
    load_poolv.start()

    def load_w(b, c):
        source = (lax.rem(b, KVH) * GQ + b // KVH) * HD
        pltpu.make_async_copy(
            w_hbm.at[pl.ds(pl.multiple_of(source, 16), HD)],
            w_v.at[pl.ds(pl.multiple_of(b * HD, 16), HD)],
            load_sem.at[5],
        ).start()
        return c

    lax.fori_loop(0, H, load_w, 0)

    load_groups.wait()
    group_row = groups[...]
    eye = iota((rows, rows), 0) == iota((rows, rows), 1)
    group_col = jnp.sum(jnp.where(eye, group_row, 0), axis=1, keepdims=True)
    earlier = (group_col == group_row) & (iota((rows, rows), 0) < iota((rows, rows), 1))
    rank = jnp.sum(earlier.astype(jnp.int32), axis=0, keepdims=True)
    slot_row = group_row * SLOTS + rank
    slot_wide = jnp.concatenate([slot_row + j * (SLOTS * n) for j in range(GQ)], axis=1)
    index = iota((n * GQ * SLOTS, 1), 0)
    offset = index // (GQ * SLOTS)
    which = index % (GQ * SLOTS)
    target = (me + offset * MIX) % n
    slot_col = (which // SLOTS) * (SLOTS * n) + target * SLOTS + which % SLOTS
    pick = (slot_col == slot_wide).astype(jnp.float32).astype(jnp.bfloat16)

    load_q.wait()
    for j in range(GQ):
        for k in range(KVH):
            piece = q_v[:, (k * GQ + j) * HD : (k * GQ + j + 1) * HD]
            qp[j * rows : (j + 1) * rows, k * HD : (k + 1) * HD] = piece
    qf[...] = qp[...].astype(jnp.float32)
    send[...] = dot(pick, qp[...]).astype(jnp.bfloat16).reshape(send.shape)

    pl.semaphore_wait(barrier, n - 1)
    pltpu.make_async_copy(send.at[0], recv.at[0], recv_sem.at[0]).start()

    def send_out(i, c):
        pltpu.make_async_remote_copy(
            src_ref=send.at[i],
            dst_ref=recv.at[i],
            send_sem=send_sem,
            recv_sem=recv_sem.at[i // per],
            device_id=(lax.rem(me + i * MIX, n),),
            device_id_type=MESH,
        ).start()
        return c

    lax.fori_loop(1, n, send_out, 0)

    rank_col = jnp.sum(jnp.where(eye, rank, 0), axis=1, keepdims=True)
    wide_col = group_col * SLOTS + rank_col
    wide_col = jnp.concatenate([wide_col + j * (SLOTS * n) for j in range(GQ)], axis=0)
    index = iota((1, n * GQ * SLOTS), 1)
    which = index % (GQ * SLOTS)
    target = (me + index // (GQ * SLOTS) * MIX) % n
    slot_line = (which // SLOTS) * (SLOTS * n) + target * SLOTS + which % SLOTS
    for c in range(CHUNKS):
        line = slot_line[:, c * (per * GQ * SLOTS) : (c + 1) * (per * GQ * SLOTS)]
        pick_back[c] = (wide_col == line).astype(jnp.float32).astype(jnp.bfloat16)

    load_pk.wait()
    load_pv.wait()
    for k in range(KVH):
        first, end = window(k)
        wide = (end - first) * LANES
        lane = iota((1, wide), 1) + first * LANES
        keep = of_head(lane, k).astype(jnp.float32).astype(jnp.bfloat16)
        kpad[k, :, :wide] = pk_v[:, first * LANES : end * LANES] * keep
        vpad[k, :, :wide] = pv_v[:, first * LANES : end * LANES] * keep

    load_table.wait()
    load_lengths.wait()
    load_poolk.wait()
    load_poolv.wait()
    lane8 = iota((KVH, KW), 1)
    block = of_head(lane8, iota((KVH, KW), 0))
    first_row = iota((2 * H, 2 * LANES), 0) < H
    token = iota((2 * H, 2 * LANES), 1) - jnp.where(first_row, 0, LANES)
    lane_row = iota((BATCH, LANES), 1)

    def private_batch(b, c):
        all_scores = []
        for u in range(0, BATCH, 2):
            parts, pages = [], []
            for r in (b * BATCH + u, b * BATCH + u + 1):
                for j in range(GQ):
                    line = qf[pl.ds(j * rows + r, 1), :]
                    parts.append(jnp.where(block, line, 0.0))
                pages.extend(poolk[table[p, r]] for p in range(PAGES))
            query = jnp.concatenate(parts, axis=0).astype(jnp.bfloat16)
            scores = dot(query, jnp.concatenate(pages, axis=0), NT)
            seen = jnp.where(first_row, lengths[b * BATCH + u], lengths[b * BATCH + u + 1])
            visible = (token >= 0) & (token < seen)
            all_scores.append(jnp.where(visible, scores, -1e30))
        scores = jnp.concatenate(all_scores, axis=0)
        largest = jnp.max(scores, axis=1, keepdims=True)
        weights = jnp.exp2((scores - largest) * (SCALE * LOG2E))
        total = jnp.sum(weights, axis=1, keepdims=True)
        share = 1.0 / total
        rounded = weights.astype(jnp.bfloat16)
        stat[...] = jnp.broadcast_to(largest * SCALE + jnp.log(total), stat.shape)
        for u in range(0, BATCH, 2):
            pages = []
            for r in (b * BATCH + u, b * BATCH + u + 1):
                pages.extend(poolv[table[p, r]] for p in range(PAGES))
            summed = dot(rounded[u * H : (u + 2) * H], jnp.concatenate(pages, axis=0))
            summed = summed * share[u * H : (u + 2) * H]
            for t in range(TILES):
                base = (t * BATCH + u) * H
                stage[base : base + 2 * H, :] = summed[:, t * LANES : (t + 1) * LANES]
        start = pl.multiple_of(b * BATCH, BATCH)
        for j in range(GQ):
            for t in range(TILES):
                lane = lane_row + t * LANES
                out = jnp.zeros((BATCH, LANES), jnp.float32)
                lse = jnp.zeros((BATCH, LANES), jnp.float32)
                for k in range(KVH):
                    first, end = window(k)
                    if first <= t < end:
                        inside = of_head(lane, k)
                        spot = pl.ds(j * KVH + k, BATCH, stride=H)
                        here = pl.ds(t * BATCH * H + j * KVH + k, BATCH, stride=H)
                        out = jnp.where(inside, stage[here, :], out)
                        lse = jnp.where(inside, stat[spot, :], lse)
                own[pl.ds(j * rows + start, BATCH), t * LANES : (t + 1) * LANES] = out
                own_lse[pl.ds(j * rows + start, BATCH), t * LANES : (t + 1) * LANES] = lse
        return c

    message = GQ * SLOTS
    span = per * message
    lane_m = iota((span, LANES), 1)

    def shared(c):
        query = recv[pl.ds(c * per, per)].reshape(span, KW)
        tiles = [None] * TILES
        lse = jnp.zeros((span, LANES), jnp.float32)
        for k in range(KVH):
            first, end = window(k)
            wide = (end - first) * LANES
            scores = dot(query[:, first * LANES : end * LANES], kpad[k, :, :wide], NT)
            largest = jnp.max(scores, axis=1, keepdims=True)
            weights = jnp.exp2((scores - largest) * (SCALE * LOG2E))
            total = jnp.sum(weights, axis=1, keepdims=True)
            summed = dot(weights.astype(jnp.bfloat16), vpad[k, :, :wide]) * (1.0 / total)
            lse = jnp.where(lane_m % KVH == k, largest * SCALE + jnp.log(total), lse)
            for t in range(first, end):
                piece = summed[:, (t - first) * LANES : (t - first + 1) * LANES]
                tiles[t] = piece if tiles[t] is None else tiles[t] + piece
        for t in range(TILES):
            result[pl.ds(c * per, per), :, t * LANES : (t + 1) * LANES] = (
                tiles[t].astype(jnp.bfloat16).reshape(per, message, LANES)
            )
        line = iota((span, LANES), 0) % message
        lse = jnp.where(lane_m // KVH == line, lse, 0.0)
        lse_out[pl.ds(c * per, per)] = jnp.sum(
            lse.reshape(per, message, LANES), axis=1, keepdims=True
        )

    def answer(i, c):
        pltpu.make_async_remote_copy(
            src_ref=result.at[i],
            dst_ref=back.at[i],
            send_sem=back_send_sem,
            recv_sem=back_sem.at[i // per],
            device_id=(lax.rem(me + i * (n - MIX), n),),
            device_id_type=MESH,
        ).start()
        return c

    def answer_lse(i, c):
        pltpu.make_async_remote_copy(
            src_ref=lse_out.at[i],
            dst_ref=lse_back.at[i],
            send_sem=lse_send_sem,
            recv_sem=lse_sem,
            device_id=(lax.rem(me + i * (n - MIX), n),),
            device_id_type=MESH,
        ).start()
        return c

    def chunk(c, carry):
        until = EARLY + EACH * c
        lax.fori_loop(jnp.where(c == 0, 0, until - EACH), until, private_batch, 0)
        arrived = recv.at[pl.ds(c * per, per)]
        pltpu.make_async_copy(arrived, arrived, recv_sem.at[c]).wait()
        shared(c)
        lax.fori_loop(jnp.maximum(c * per, 1), (c + 1) * per, answer_lse, 0)
        lax.fori_loop(jnp.maximum(c * per, 1), (c + 1) * per, answer, 0)
        return carry

    lax.fori_loop(0, CHUNKS, chunk, 0)
    pltpu.make_async_copy(result.at[0], back.at[0], back_sem.at[0]).start()
    pltpu.make_async_copy(lse_out.at[0], lse_back.at[0], lse_sem).start()
    lax.fori_loop(EARLY + EACH * (CHUNKS - 1), rows // BATCH, private_batch, 0)

    others = send.at[pl.ds(1, n - 1)]
    pltpu.make_async_copy(others, others, send_sem).wait()
    pltpu.make_async_copy(w_v, w_v, load_sem.at[5]).wait()

    others = lse_out.at[pl.ds(1, n - 1)]
    pltpu.make_async_copy(others, others, lse_send_sem).wait()
    pltpu.make_async_copy(lse_back, lse_back, lse_sem).wait()
    used = GQ * SLOTS * KVH
    lse = lse_back[...].reshape(n, LANES)[:, :used]
    high = lse.astype(jnp.bfloat16).astype(jnp.float32)
    rest = lse - high
    middle = rest.astype(jnp.bfloat16).astype(jnp.float32)
    three = jnp.concatenate([high, middle, rest - middle, jnp.zeros_like(high)], axis=1)
    from_group = (group_col == (me + iota((rows, n), 1) * MIX) % n)
    from_group = from_group.astype(jnp.float32).astype(jnp.bfloat16)
    lines = dot(from_group, three.astype(jnp.bfloat16))
    lane3 = iota((rows, 4 * used), 1)
    mine = lane3 // KVH % SLOTS == rank_col
    lines = jnp.concatenate(
        [
            jnp.where(mine & (lane3 % used // (KVH * SLOTS) == j), lines, 0.0)
            for j in range(GQ)
        ],
        axis=0,
    )
    expand = of_head(iota((4 * used, KW), 1), iota((4 * used, KW), 0) % KVH)
    expand = expand.astype(jnp.float32).astype(jnp.bfloat16)
    prefix_lse = dot(lines.astype(jnp.bfloat16), expand)
    private_lse = own_lse[...]
    most = jnp.maximum(prefix_lse, private_lse)
    a = jnp.exp(prefix_lse - most)
    b = jnp.exp(private_lse - most)
    both = 1.0 / (a + b)
    own[...] = own[...] * (b * both)
    own_lse[...] = a * both

    def returned_rows(c):
        returned = back.at[pl.ds(c * per, per)]
        pltpu.make_async_copy(returned, returned, back_sem.at[c]).wait()
        return dot(pick_back[c], back[pl.ds(c * per, per)].reshape(span, KW))

    def gather(c, carry):
        spread[...] += returned_rows(c)
        return carry

    spread[...] = returned_rows(0)
    lax.fori_loop(1, CHUNKS - 1, gather, 0)
    others = result.at[pl.ds(1, n - 1)]
    pltpu.make_async_copy(others, others, back_send_sem).wait()
    prefix_out = spread[...] + returned_rows(CHUNKS - 1)
    attended = (own_lse[...] * prefix_out + own[...]).astype(jnp.bfloat16)
    flat = jnp.concatenate([attended[j * rows : (j + 1) * rows] for j in range(GQ)], axis=1)
    width = 512
    for t in range(o_ref.shape[1] // width):
        projected = dot(flat, w_v[:, t * width : (t + 1) * width])
        o_ref[:, t * width : (t + 1) * width] = projected.astype(jnp.bfloat16)


def per_device(
    queries,
    prefix_keys,
    prefix_values,
    pool_keys,
    pool_values,
    page_table,
    private_length,
    group_ids,
    live_rows,
    out_weight,
):
    n = lax.axis_size("req")
    rows, width = queries.shape
    tokens = prefix_keys.shape[0]
    message = GQ * SLOTS
    bf16, f32 = jnp.bfloat16, jnp.float32
    vmem = pl.BlockSpec(memory_space=pltpu.VMEM)
    far = pl.BlockSpec(memory_space=pltpu.HBM)
    projected = pl.pallas_call(
        functools.partial(kernel, n, rows),
        out_shape=jax.ShapeDtypeStruct((rows, width), bf16),
        in_specs=[far] * 9,
        out_specs=vmem,
        scratch_shapes=[
            pltpu.SMEM(page_table.shape[::-1], jnp.int32),
            pltpu.SMEM(private_length.shape, jnp.int32),
            pltpu.VMEM((1, rows), jnp.int32),
            pltpu.VMEM(queries.shape, bf16),
            pltpu.VMEM(prefix_keys.shape, bf16),
            pltpu.VMEM(prefix_values.shape, bf16),
            pltpu.VMEM(pool_keys.shape, bf16),
            pltpu.VMEM(pool_values.shape, bf16),
            pltpu.VMEM(out_weight.shape, bf16),
            pltpu.VMEM((GQ * rows, KW), bf16),
            pltpu.VMEM((GQ * rows, KW), f32),
            pltpu.VMEM((KVH, tokens, 2 * LANES), bf16),
            pltpu.VMEM((KVH, tokens, 2 * LANES), bf16),
            pltpu.VMEM((n, message, KW), bf16),
            pltpu.VMEM((n, message, KW), bf16),
            pltpu.VMEM((n, message, KW), bf16),
            pltpu.VMEM((n, message, KW), bf16),
            pltpu.VMEM((n, 1, LANES), f32),
            pltpu.VMEM((n, 1, LANES), f32),
            pltpu.VMEM((TILES * BATCH * H, LANES), f32),
            pltpu.VMEM((BATCH * H, LANES), f32),
            pltpu.VMEM((GQ * rows, KW), f32),
            pltpu.VMEM((GQ * rows, KW), f32),
            pltpu.VMEM((CHUNKS, GQ * rows, n * message // CHUNKS), bf16),
            pltpu.VMEM((GQ * rows, KW), f32),
            pltpu.SemaphoreType.DMA((9,)),
            pltpu.SemaphoreType.DMA,
            pltpu.SemaphoreType.DMA((CHUNKS,)),
            pltpu.SemaphoreType.DMA,
            pltpu.SemaphoreType.DMA((CHUNKS,)),
            pltpu.SemaphoreType.DMA,
            pltpu.SemaphoreType.DMA,
        ],
        compiler_params=pltpu.CompilerParams(
            collective_id=0, has_side_effects=True, vmem_limit_bytes=48 << 20
        ),
    )(
        *(
            pltpu.with_memory_space_constraint(x, pltpu.HBM)
            for x in (
                page_table.T,
                private_length,
                group_ids.reshape(1, rows),
                queries,
                prefix_keys,
                prefix_values,
                pool_keys,
                pool_values,
                out_weight,
            )
        )
    )
    is_live = jnp.arange(rows, dtype=jnp.int32)[:, None] < live_rows[0]
    return jnp.where(is_live, projected, jnp.zeros_like(projected))


def solution(mesh):
    placed = (
        P("req", None),
        P("req", None),
        P("req", None),
        P("req", None, None),
        P("req", None, None),
        P("req", None),
        P("req"),
        P("req", None),
        P("req"),
        P(),
    )
    return jax.shard_map(
        per_device, mesh=mesh, in_specs=placed, out_specs=P("req", None), check_vma=False
    )
```

```python
import functools

import jax
import jax.numpy as jnp
from jax import lax
from jax.experimental import pallas as pl
from jax.experimental.pallas import tpu as pltpu
from jax.sharding import PartitionSpec as P

MESH = pl.DeviceIdType.MESH
H = 32
KVH = 8
HD = 80
GQ = H // KVH
KW = KVH * HD
LANES = 128
TILES = KW // LANES
SLOTS = 2
MIX = 45
CHUNKS = 4
SPLIT = 2
CUT = 3 * LANES
BATCH = 16
PAGES = 8
EARLY = 2
EACH = 1
SCALE = HD ** (-0.5)
LOG2E = 1.4426950408889634
NT = (((1,), (1,)), ((), ()))
NN = (((1,), (0,)), ((), ()))


def dot(a, b, dims=NN):
    return lax.dot_general(a, b, dims, preferred_element_type=jnp.float32)


def iota(shape, axis):
    return lax.broadcasted_iota(jnp.int32, shape, axis)


def window(k):
    first = k * HD // LANES
    last = (k * HD + HD - 1) // LANES
    return first, last + 1


def of_head(lane, k):
    return (lane >= k * HD) & (lane < (k + 1) * HD)


def kernel(
    n,
    rows,
    table_hbm,
    lengths_hbm,
    groups_hbm,
    q_hbm,
    pk_hbm,
    pv_hbm,
    poolk_hbm,
    poolv_hbm,
    w_hbm,
    o_ref,
    table,
    lengths,
    groups,
    q_v,
    pk_v,
    pv_v,
    poolk,
    poolv,
    w_v,
    qp,
    qf,
    kpad,
    vpad,
    send,
    recv,
    result,
    back,
    lse_out,
    lse_back,
    stage,
    stat,
    own,
    own_lse,
    pick_back,
    spread,
    half,
    load_sem,
    send_sem,
    recv_sem,
    back_send_sem,
    back_sem,
    lse_send_sem,
    lse_sem,
):
    me = lax.axis_index("req")
    per = n // CHUNKS
    load_q = pltpu.make_async_copy(q_hbm, q_v, load_sem.at[0])
    load_pk = pltpu.make_async_copy(pk_hbm, pk_v, load_sem.at[1])
    load_pv = pltpu.make_async_copy(pv_hbm, pv_v, load_sem.at[2])
    load_poolk = pltpu.make_async_copy(poolk_hbm, poolk, load_sem.at[3])
    load_poolv = pltpu.make_async_copy(poolv_hbm, poolv, load_sem.at[4])
    load_table = pltpu.make_async_copy(table_hbm, table, load_sem.at[6])
    load_lengths = pltpu.make_async_copy(lengths_hbm, lengths, load_sem.at[7])
    load_groups = pltpu.make_async_copy(groups_hbm, groups, load_sem.at[8])
    load_groups.start()
    load_q.start()
    load_table.start()
    load_lengths.start()
    barrier = pltpu.get_barrier_semaphore()

    def greet(i, c):
        pl.semaphore_signal(
            barrier, inc=1, device_id=(lax.rem(me + i, n),), device_id_type=MESH
        )
        return c

    lax.fori_loop(1, n, greet, 0, unroll=8)
    load_pk.start()
    load_pv.start()
    load_poolk.start()
    load_poolv.start()

    def load_w(b, c):
        source = (lax.rem(b, KVH) * GQ + b // KVH) * HD
        pltpu.make_async_copy(
            w_hbm.at[pl.ds(pl.multiple_of(source, 16), HD)],
            w_v.at[pl.ds(pl.multiple_of(b * HD, 16), HD)],
            load_sem.at[5],
        ).start()
        return c

    lax.fori_loop(0, H, load_w, 0)

    load_groups.wait()
    group_row = groups[...]
    eye = iota((rows, rows), 0) == iota((rows, rows), 1)
    group_col = jnp.sum(jnp.where(eye, group_row, 0), axis=1, keepdims=True)
    earlier = (group_col == group_row) & (iota((rows, rows), 0) < iota((rows, rows), 1))
    rank = jnp.sum(earlier.astype(jnp.int32), axis=0, keepdims=True)
    slot_row = group_row * SLOTS + rank
    slot_wide = jnp.concatenate([slot_row + j * (SLOTS * n) for j in range(GQ)], axis=1)
    index = iota((n * GQ * SLOTS, 1), 0)
    offset = index // (GQ * SLOTS)
    which = index % (GQ * SLOTS)
    target = (me + offset * MIX) % n
    slot_col = (which // SLOTS) * (SLOTS * n) + target * SLOTS + which % SLOTS
    pick = (slot_col == slot_wide).astype(jnp.float32).astype(jnp.bfloat16)

    load_q.wait()
    for j in range(GQ):
        for k in range(KVH):
            piece = q_v[:, (k * GQ + j) * HD : (k * GQ + j + 1) * HD]
            qp[j * rows : (j + 1) * rows, k * HD : (k + 1) * HD] = piece
    qf[...] = qp[...].astype(jnp.float32)
    send[...] = dot(pick, qp[...]).astype(jnp.bfloat16).reshape(send.shape)

    pl.semaphore_wait(barrier, n - 1)
    pltpu.make_async_copy(send.at[0], recv.at[0], recv_sem.at[0]).start()

    def send_out(i, c):
        pltpu.make_async_remote_copy(
            src_ref=send.at[i],
            dst_ref=recv.at[i],
            send_sem=send_sem,
            recv_sem=recv_sem.at[i // per],
            device_id=(lax.rem(me + i * MIX, n),),
            device_id_type=MESH,
        ).start()
        return c

    lax.fori_loop(1, n, send_out, 0)

    rank_col = jnp.sum(jnp.where(eye, rank, 0), axis=1, keepdims=True)
    wide_col = group_col * SLOTS + rank_col
    wide_col = jnp.concatenate([wide_col + j * (SLOTS * n) for j in range(GQ)], axis=0)
    index = iota((1, n * GQ * SLOTS), 1)
    which = index % (GQ * SLOTS)
    target = (me + index // (GQ * SLOTS) * MIX) % n
    slot_line = (which // SLOTS) * (SLOTS * n) + target * SLOTS + which % SLOTS
    for c in range(CHUNKS):
        line = slot_line[:, c * (per * GQ * SLOTS) : (c + 1) * (per * GQ * SLOTS)]
        pick_back[c] = (wide_col == line).astype(jnp.float32).astype(jnp.bfloat16)

    load_pk.wait()
    load_pv.wait()
    for k in range(KVH):
        first, end = window(k)
        wide = (end - first) * LANES
        lane = iota((1, wide), 1) + first * LANES
        keep = of_head(lane, k).astype(jnp.float32).astype(jnp.bfloat16)
        kpad[k, :, :wide] = pk_v[:, first * LANES : end * LANES] * keep
        vpad[k, :, :wide] = pv_v[:, first * LANES : end * LANES] * keep

    load_table.wait()
    load_lengths.wait()
    load_poolk.wait()
    load_poolv.wait()
    lane8 = iota((KVH, KW), 1)
    block = of_head(lane8, iota((KVH, KW), 0))
    first_row = iota((2 * H, 2 * LANES), 0) < H
    token = iota((2 * H, 2 * LANES), 1) - jnp.where(first_row, 0, LANES)
    lane_row = iota((BATCH, LANES), 1)

    def private_batch(b, c):
        all_scores = []
        for u in range(0, BATCH, 2):
            parts, pages = [], []
            for r in (b * BATCH + u, b * BATCH + u + 1):
                for j in range(GQ):
                    line = qf[pl.ds(j * rows + r, 1), :]
                    parts.append(jnp.where(block, line, 0.0))
                pages.extend(poolk[table[p, r]] for p in range(PAGES))
            query = jnp.concatenate(parts, axis=0).astype(jnp.bfloat16)
            scores = dot(query, jnp.concatenate(pages, axis=0), NT)
            seen = jnp.where(first_row, lengths[b * BATCH + u], lengths[b * BATCH + u + 1])
            visible = (token >= 0) & (token < seen)
            all_scores.append(jnp.where(visible, scores, -1e30))
        scores = jnp.concatenate(all_scores, axis=0)
        largest = jnp.max(scores, axis=1, keepdims=True)
        weights = jnp.exp2((scores - largest) * (SCALE * LOG2E))
        total = jnp.sum(weights, axis=1, keepdims=True)
        share = 1.0 / total
        rounded = weights.astype(jnp.bfloat16)
        stat[...] = jnp.broadcast_to(largest * SCALE + jnp.log(total), stat.shape)
        for u in range(0, BATCH, 2):
            pages = []
            for r in (b * BATCH + u, b * BATCH + u + 1):
                pages.extend(poolv[table[p, r]] for p in range(PAGES))
            summed = dot(rounded[u * H : (u + 2) * H], jnp.concatenate(pages, axis=0))
            summed = summed * share[u * H : (u + 2) * H]
            for t in range(TILES):
                base = (t * BATCH + u) * H
                stage[base : base + 2 * H, :] = summed[:, t * LANES : (t + 1) * LANES]
        start = pl.multiple_of(b * BATCH, BATCH)
        for j in range(GQ):
            for t in range(TILES):
                lane = lane_row + t * LANES
                out = jnp.zeros((BATCH, LANES), jnp.float32)
                lse = jnp.zeros((BATCH, LANES), jnp.float32)
                for k in range(KVH):
                    first, end = window(k)
                    if first <= t < end:
                        inside = of_head(lane, k)
                        spot = pl.ds(j * KVH + k, BATCH, stride=H)
                        here = pl.ds(t * BATCH * H + j * KVH + k, BATCH, stride=H)
                        out = jnp.where(inside, stage[here, :], out)
                        lse = jnp.where(inside, stat[spot, :], lse)
                own[pl.ds(j * rows + start, BATCH), t * LANES : (t + 1) * LANES] = out
                own_lse[pl.ds(j * rows + start, BATCH), t * LANES : (t + 1) * LANES] = lse
        return c

    message = GQ * SLOTS
    span = per * message
    lane_m = iota((span, LANES), 1)

    def shared(c):
        query = recv[pl.ds(c * per, per)].reshape(span, KW)
        tiles = [None] * TILES
        lse = jnp.zeros((span, LANES), jnp.float32)
        for k in range(KVH):
            first, end = window(k)
            wide = (end - first) * LANES
            scores = dot(query[:, first * LANES : end * LANES], kpad[k, :, :wide], NT)
            largest = jnp.max(scores, axis=1, keepdims=True)
            weights = jnp.exp2((scores - largest) * (SCALE * LOG2E))
            total = jnp.sum(weights, axis=1, keepdims=True)
            summed = dot(weights.astype(jnp.bfloat16), vpad[k, :, :wide]) * (1.0 / total)
            lse = jnp.where(lane_m % KVH == k, largest * SCALE + jnp.log(total), lse)
            for t in range(first, end):
                piece = summed[:, (t - first) * LANES : (t - first + 1) * LANES]
                tiles[t] = piece if tiles[t] is None else tiles[t] + piece
        for t in range(TILES):
            result[pl.ds(c * per, per), :, t * LANES : (t + 1) * LANES] = (
                tiles[t].astype(jnp.bfloat16).reshape(per, message, LANES)
            )
        line = iota((span, LANES), 0) % message
        lse = jnp.where(lane_m // KVH == line, lse, 0.0)
        lse_out[pl.ds(c * per, per)] = jnp.sum(
            lse.reshape(per, message, LANES), axis=1, keepdims=True
        )

    def answer(c, low, high, arrival):
        def send_back(i, carry):
            pltpu.make_async_remote_copy(
                src_ref=result.at[i, :, pl.ds(low, high - low)],
                dst_ref=back.at[i, :, pl.ds(low, high - low)],
                send_sem=back_send_sem,
                recv_sem=back_sem.at[arrival],
                device_id=(lax.rem(me + i * (n - MIX), n),),
                device_id_type=MESH,
            ).start()
            return carry

        lax.fori_loop(jnp.maximum(c * per, 1), (c + 1) * per, send_back, 0)

    def answer_lse(i, c):
        pltpu.make_async_remote_copy(
            src_ref=lse_out.at[i],
            dst_ref=lse_back.at[i],
            send_sem=lse_send_sem,
            recv_sem=lse_sem,
            device_id=(lax.rem(me + i * (n - MIX), n),),
            device_id_type=MESH,
        ).start()
        return c

    def chunk(c, carry):
        until = EARLY + EACH * c
        lax.fori_loop(jnp.where(c == 0, 0, until - EACH), until, private_batch, 0)
        arrived = recv.at[pl.ds(c * per, per)]
        pltpu.make_async_copy(arrived, arrived, recv_sem.at[c]).wait()
        shared(c)
        lax.fori_loop(jnp.maximum(c * per, 1), (c + 1) * per, answer_lse, 0)

        @pl.when(c < CHUNKS - SPLIT)
        def _():
            answer(c, 0, KW, c)

        @pl.when(c >= CHUNKS - SPLIT)
        def _():
            answer(c, 0, CUT, c)

        return carry

    lax.fori_loop(0, CHUNKS, chunk, 0)
    for c in range(CHUNKS - SPLIT, CHUNKS):
        answer(c, CUT, KW, c + SPLIT)
    pltpu.make_async_copy(result.at[0], back.at[0], back_sem.at[0]).start()
    pltpu.make_async_copy(lse_out.at[0], lse_back.at[0], lse_sem).start()
    lax.fori_loop(EARLY + EACH * (CHUNKS - 1), rows // BATCH, private_batch, 0)

    others = send.at[pl.ds(1, n - 1)]
    pltpu.make_async_copy(others, others, send_sem).wait()
    pltpu.make_async_copy(w_v, w_v, load_sem.at[5]).wait()

    others = lse_out.at[pl.ds(1, n - 1)]
    pltpu.make_async_copy(others, others, lse_send_sem).wait()
    pltpu.make_async_copy(lse_back, lse_back, lse_sem).wait()
    used = GQ * SLOTS * KVH
    lse = lse_back[...].reshape(n, LANES)[:, :used]
    high = lse.astype(jnp.bfloat16).astype(jnp.float32)
    rest = lse - high
    middle = rest.astype(jnp.bfloat16).astype(jnp.float32)
    three = jnp.concatenate([high, middle, rest - middle, jnp.zeros_like(high)], axis=1)
    from_group = (group_col == (me + iota((rows, n), 1) * MIX) % n)
    from_group = from_group.astype(jnp.float32).astype(jnp.bfloat16)
    lines = dot(from_group, three.astype(jnp.bfloat16))
    lane3 = iota((rows, 4 * used), 1)
    mine = lane3 // KVH % SLOTS == rank_col
    lines = jnp.concatenate(
        [
            jnp.where(mine & (lane3 % used // (KVH * SLOTS) == j), lines, 0.0)
            for j in range(GQ)
        ],
        axis=0,
    )
    expand = of_head(iota((4 * used, KW), 1), iota((4 * used, KW), 0) % KVH)
    expand = expand.astype(jnp.float32).astype(jnp.bfloat16)
    prefix_lse = dot(lines.astype(jnp.bfloat16), expand)
    private_lse = own_lse[...]
    most = jnp.maximum(prefix_lse, private_lse)
    a = jnp.exp(prefix_lse - most)
    b = jnp.exp(private_lse - most)
    both = 1.0 / (a + b)
    own[...] = own[...] * (b * both)
    own_lse[...] = a * both

    def returned_rows(c, low, high, arrival):
        returned = back.at[pl.ds(c * per, per), :, pl.ds(low, high - low)]
        pltpu.make_async_copy(returned, returned, back_sem.at[arrival]).wait()
        arrived = back[pl.ds(c * per, per), :, low:high].reshape(span, high - low)
        return dot(pick_back[c], arrived)

    def gather(c, carry):
        spread[...] += returned_rows(c, 0, KW, c)
        return carry

    spread[...] = returned_rows(0, 0, KW, 0)
    lax.fori_loop(1, CHUNKS - SPLIT, gather, 0)
    width = 512
    for low, high, late in ((0, CUT, 0), (CUT, KW, SPLIT)):
        prefix_out = spread[:, low:high]
        for c in range(CHUNKS - SPLIT, CHUNKS):
            prefix_out = prefix_out + returned_rows(c, low, high, c + late)
        attended = own_lse[:, low:high] * prefix_out + own[:, low:high]
        attended = attended.astype(jnp.bfloat16)
        for t in range(o_ref.shape[1] // width):
            columns = slice(t * width, (t + 1) * width)
            part = None
            for j in range(GQ):
                term = dot(
                    attended[j * rows : (j + 1) * rows],
                    w_v[j * KW + low : j * KW + high, columns],
                )
                part = term if part is None else part + term
            if late:
                o_ref[:, columns] = (half[:, columns] + part).astype(jnp.bfloat16)
            else:
                half[:, columns] = part
    others = result.at[pl.ds(1, n - 1)]
    pltpu.make_async_copy(others, others, back_send_sem).wait()


def per_device(
    queries,
    prefix_keys,
    prefix_values,
    pool_keys,
    pool_values,
    page_table,
    private_length,
    group_ids,
    live_rows,
    out_weight,
):
    n = lax.axis_size("req")
    rows, width = queries.shape
    tokens = prefix_keys.shape[0]
    message = GQ * SLOTS
    bf16, f32 = jnp.bfloat16, jnp.float32
    vmem = pl.BlockSpec(memory_space=pltpu.VMEM)
    far = pl.BlockSpec(memory_space=pltpu.HBM)
    projected = pl.pallas_call(
        functools.partial(kernel, n, rows),
        out_shape=jax.ShapeDtypeStruct((rows, width), bf16),
        in_specs=[far] * 9,
        out_specs=vmem,
        scratch_shapes=[
            pltpu.SMEM(page_table.shape[::-1], jnp.int32),
            pltpu.SMEM(private_length.shape, jnp.int32),
            pltpu.VMEM((1, rows), jnp.int32),
            pltpu.VMEM(queries.shape, bf16),
            pltpu.VMEM(prefix_keys.shape, bf16),
            pltpu.VMEM(prefix_values.shape, bf16),
            pltpu.VMEM(pool_keys.shape, bf16),
            pltpu.VMEM(pool_values.shape, bf16),
            pltpu.VMEM(out_weight.shape, bf16),
            pltpu.VMEM((GQ * rows, KW), bf16),
            pltpu.VMEM((GQ * rows, KW), f32),
            pltpu.VMEM((KVH, tokens, 2 * LANES), bf16),
            pltpu.VMEM((KVH, tokens, 2 * LANES), bf16),
            pltpu.VMEM((n, message, KW), bf16),
            pltpu.VMEM((n, message, KW), bf16),
            pltpu.VMEM((n, message, KW), bf16),
            pltpu.VMEM((n, message, KW), bf16),
            pltpu.VMEM((n, 1, LANES), f32),
            pltpu.VMEM((n, 1, LANES), f32),
            pltpu.VMEM((TILES * BATCH * H, LANES), f32),
            pltpu.VMEM((BATCH * H, LANES), f32),
            pltpu.VMEM((GQ * rows, KW), f32),
            pltpu.VMEM((GQ * rows, KW), f32),
            pltpu.VMEM((CHUNKS, GQ * rows, n * message // CHUNKS), bf16),
            pltpu.VMEM((GQ * rows, KW), f32),
            pltpu.VMEM((rows, width), f32),
            pltpu.SemaphoreType.DMA((9,)),
            pltpu.SemaphoreType.DMA,
            pltpu.SemaphoreType.DMA((CHUNKS,)),
            pltpu.SemaphoreType.DMA,
            pltpu.SemaphoreType.DMA((CHUNKS + SPLIT,)),
            pltpu.SemaphoreType.DMA,
            pltpu.SemaphoreType.DMA,
        ],
        compiler_params=pltpu.CompilerParams(
            collective_id=0, has_side_effects=True, vmem_limit_bytes=48 << 20
        ),
    )(
        *(
            pltpu.with_memory_space_constraint(x, pltpu.HBM)
            for x in (
                page_table.T,
                private_length,
                group_ids.reshape(1, rows),
                queries,
                prefix_keys,
                prefix_values,
                pool_keys,
                pool_values,
                out_weight,
            )
        )
    )
    is_live = jnp.arange(rows, dtype=jnp.int32)[:, None] < live_rows[0]
    return jnp.where(is_live, projected, jnp.zeros_like(projected))


def solution(mesh):
    placed = (
        P("req", None),
        P("req", None),
        P("req", None),
        P("req", None, None),
        P("req", None, None),
        P("req", None),
        P("req"),
        P("req", None),
        P("req"),
        P(),
    )
    return jax.shard_map(
        per_device, mesh=mesh, in_specs=placed, out_specs=P("req", None), check_vma=False
    )
```

```python
import functools

import jax
import jax.numpy as jnp
from jax import lax
from jax.experimental import pallas as pl
from jax.experimental.pallas import tpu as pltpu
from jax.sharding import PartitionSpec as P

MESH = pl.DeviceIdType.MESH
H = 32
KVH = 8
HD = 80
GQ = H // KVH
KW = KVH * HD
LANES = 128
TILES = KW // LANES
SLOTS = 2
MIX = 43
CHUNKS = 4
SPLIT = 2
CUT = 3 * LANES
BATCH = 16
PAGES = 8
EARLY = 2
EACH = 1
SCALE = HD ** (-0.5)
LOG2E = 1.4426950408889634
NT = (((1,), (1,)), ((), ()))
NN = (((1,), (0,)), ((), ()))


def dot(a, b, dims=NN):
    return lax.dot_general(a, b, dims, preferred_element_type=jnp.float32)


def iota(shape, axis):
    return lax.broadcasted_iota(jnp.int32, shape, axis)


def window(k):
    first = k * HD // LANES
    last = (k * HD + HD - 1) // LANES
    return first, last + 1


def of_head(lane, k):
    return (lane >= k * HD) & (lane < (k + 1) * HD)


def kernel(
    n,
    rows,
    table_hbm,
    lengths_hbm,
    groups_hbm,
    q_hbm,
    pk_hbm,
    pv_hbm,
    poolk_hbm,
    poolv_hbm,
    w_hbm,
    o_ref,
    table,
    lengths,
    groups,
    q_v,
    pk_v,
    pv_v,
    poolk,
    poolv,
    w_v,
    qp,
    qf,
    kpad,
    vpad,
    send,
    recv,
    result,
    back,
    lse_out,
    lse_back,
    stage,
    stat,
    own,
    own_lse,
    pick_back,
    spread,
    half,
    load_sem,
    send_sem,
    recv_sem,
    back_send_sem,
    back_sem,
    lse_send_sem,
    lse_sem,
):
    me = lax.axis_index("req")
    per = n // CHUNKS
    load_q = pltpu.make_async_copy(q_hbm, q_v, load_sem.at[0])
    load_pk = pltpu.make_async_copy(pk_hbm, pk_v, load_sem.at[1])
    load_pv = pltpu.make_async_copy(pv_hbm, pv_v, load_sem.at[2])
    load_poolk = pltpu.make_async_copy(poolk_hbm, poolk, load_sem.at[3])
    load_poolv = pltpu.make_async_copy(poolv_hbm, poolv, load_sem.at[4])
    load_table = pltpu.make_async_copy(table_hbm, table, load_sem.at[6])
    load_lengths = pltpu.make_async_copy(lengths_hbm, lengths, load_sem.at[7])
    load_groups = pltpu.make_async_copy(groups_hbm, groups, load_sem.at[8])
    load_groups.start()
    load_q.start()
    load_table.start()
    load_lengths.start()
    barrier = pltpu.get_barrier_semaphore()

    def greet(i, c):
        pl.semaphore_signal(
            barrier, inc=1, device_id=(lax.rem(me + i, n),), device_id_type=MESH
        )
        return c

    lax.fori_loop(1, n, greet, 0, unroll=8)
    load_pk.start()
    load_pv.start()
    load_poolk.start()
    load_poolv.start()

    def load_w(b, c):
        source = (lax.rem(b, KVH) * GQ + b // KVH) * HD
        pltpu.make_async_copy(
            w_hbm.at[pl.ds(pl.multiple_of(source, 16), HD)],
            w_v.at[pl.ds(pl.multiple_of(b * HD, 16), HD)],
            load_sem.at[5],
        ).start()
        return c

    lax.fori_loop(0, H, load_w, 0)

    load_groups.wait()
    group_row = groups[...]
    eye = iota((rows, rows), 0) == iota((rows, rows), 1)
    group_col = jnp.sum(jnp.where(eye, group_row, 0), axis=1, keepdims=True)
    earlier = (group_col == group_row) & (iota((rows, rows), 0) < iota((rows, rows), 1))
    rank = jnp.sum(earlier.astype(jnp.int32), axis=0, keepdims=True)
    slot_row = group_row * SLOTS + rank
    slot_wide = jnp.concatenate([slot_row + j * (SLOTS * n) for j in range(GQ)], axis=1)
    index = iota((n * GQ * SLOTS, 1), 0)
    offset = index // (GQ * SLOTS)
    which = index % (GQ * SLOTS)
    target = (me + offset * MIX) % n
    slot_col = (which // SLOTS) * (SLOTS * n) + target * SLOTS + which % SLOTS
    pick = (slot_col == slot_wide).astype(jnp.float32).astype(jnp.bfloat16)

    load_q.wait()
    for j in range(GQ):
        for k in range(KVH):
            piece = q_v[:, (k * GQ + j) * HD : (k * GQ + j + 1) * HD]
            qp[j * rows : (j + 1) * rows, k * HD : (k + 1) * HD] = piece
    qf[...] = qp[...].astype(jnp.float32)
    send[...] = dot(pick, qp[...]).astype(jnp.bfloat16).reshape(send.shape)

    pl.semaphore_wait(barrier, n - 1)
    pltpu.make_async_copy(send.at[0], recv.at[0], recv_sem.at[0]).start()

    def send_out(i, c):
        pltpu.make_async_remote_copy(
            src_ref=send.at[i],
            dst_ref=recv.at[i],
            send_sem=send_sem,
            recv_sem=recv_sem.at[i // per],
            device_id=(lax.rem(me + i * MIX, n),),
            device_id_type=MESH,
        ).start()
        return c

    lax.fori_loop(1, n, send_out, 0)

    rank_col = jnp.sum(jnp.where(eye, rank, 0), axis=1, keepdims=True)
    wide_col = group_col * SLOTS + rank_col
    wide_col = jnp.concatenate([wide_col + j * (SLOTS * n) for j in range(GQ)], axis=0)
    index = iota((1, n * GQ * SLOTS), 1)
    which = index % (GQ * SLOTS)
    target = (me + index // (GQ * SLOTS) * MIX) % n
    slot_line = (which // SLOTS) * (SLOTS * n) + target * SLOTS + which % SLOTS
    for c in range(CHUNKS):
        line = slot_line[:, c * (per * GQ * SLOTS) : (c + 1) * (per * GQ * SLOTS)]
        pick_back[c] = (wide_col == line).astype(jnp.float32).astype(jnp.bfloat16)

    load_pk.wait()
    load_pv.wait()
    for k in range(KVH):
        first, end = window(k)
        wide = (end - first) * LANES
        lane = iota((1, wide), 1) + first * LANES
        keep = of_head(lane, k).astype(jnp.float32).astype(jnp.bfloat16)
        kpad[k, :, :wide] = pk_v[:, first * LANES : end * LANES] * keep
        vpad[k, :, :wide] = pv_v[:, first * LANES : end * LANES] * keep

    load_table.wait()
    load_lengths.wait()
    load_poolk.wait()
    load_poolv.wait()
    lane8 = iota((KVH, KW), 1)
    block = of_head(lane8, iota((KVH, KW), 0))
    first_row = iota((2 * H, 2 * LANES), 0) < H
    token = iota((2 * H, 2 * LANES), 1) - jnp.where(first_row, 0, LANES)
    lane_row = iota((BATCH, LANES), 1)

    def private_batch(b, c):
        all_scores = []
        for u in range(0, BATCH, 2):
            parts, pages = [], []
            for r in (b * BATCH + u, b * BATCH + u + 1):
                for j in range(GQ):
                    line = qf[pl.ds(j * rows + r, 1), :]
                    parts.append(jnp.where(block, line, 0.0))
                pages.extend(poolk[table[p, r]] for p in range(PAGES))
            query = jnp.concatenate(parts, axis=0).astype(jnp.bfloat16)
            scores = dot(query, jnp.concatenate(pages, axis=0), NT)
            seen = jnp.where(first_row, lengths[b * BATCH + u], lengths[b * BATCH + u + 1])
            visible = (token >= 0) & (token < seen)
            all_scores.append(jnp.where(visible, scores, -1e30))
        scores = jnp.concatenate(all_scores, axis=0)
        largest = jnp.max(scores, axis=1, keepdims=True)
        weights = jnp.exp2((scores - largest) * (SCALE * LOG2E))
        total = jnp.sum(weights, axis=1, keepdims=True)
        share = 1.0 / total
        rounded = weights.astype(jnp.bfloat16)
        stat[...] = jnp.broadcast_to(largest * SCALE + jnp.log(total), stat.shape)
        for u in range(0, BATCH, 2):
            pages = []
            for r in (b * BATCH + u, b * BATCH + u + 1):
                pages.extend(poolv[table[p, r]] for p in range(PAGES))
            summed = dot(rounded[u * H : (u + 2) * H], jnp.concatenate(pages, axis=0))
            summed = summed * share[u * H : (u + 2) * H]
            for t in range(TILES):
                base = (t * BATCH + u) * H
                stage[base : base + 2 * H, :] = summed[:, t * LANES : (t + 1) * LANES]
        start = pl.multiple_of(b * BATCH, BATCH)
        for j in range(GQ):
            for t in range(TILES):
                lane = lane_row + t * LANES
                out = jnp.zeros((BATCH, LANES), jnp.float32)
                lse = jnp.zeros((BATCH, LANES), jnp.float32)
                for k in range(KVH):
                    first, end = window(k)
                    if first <= t < end:
                        inside = of_head(lane, k)
                        spot = pl.ds(j * KVH + k, BATCH, stride=H)
                        here = pl.ds(t * BATCH * H + j * KVH + k, BATCH, stride=H)
                        out = jnp.where(inside, stage[here, :], out)
                        lse = jnp.where(inside, stat[spot, :], lse)
                own[pl.ds(j * rows + start, BATCH), t * LANES : (t + 1) * LANES] = out
                own_lse[pl.ds(j * rows + start, BATCH), t * LANES : (t + 1) * LANES] = lse
        return c

    message = GQ * SLOTS
    span = per * message
    lane_m = iota((span, LANES), 1)

    def shared(c):
        query = recv[pl.ds(c * per, per)].reshape(span, KW)
        tiles = [None] * TILES
        lse = jnp.zeros((span, LANES), jnp.float32)
        for k in range(KVH):
            first, end = window(k)
            wide = (end - first) * LANES
            scores = dot(query[:, first * LANES : end * LANES], kpad[k, :, :wide], NT)
            largest = jnp.max(scores, axis=1, keepdims=True)
            weights = jnp.exp2((scores - largest) * (SCALE * LOG2E))
            total = jnp.sum(weights, axis=1, keepdims=True)
            summed = dot(weights.astype(jnp.bfloat16), vpad[k, :, :wide]) * (1.0 / total)
            lse = jnp.where(lane_m % KVH == k, largest * SCALE + jnp.log(total), lse)
            for t in range(first, end):
                piece = summed[:, (t - first) * LANES : (t - first + 1) * LANES]
                tiles[t] = piece if tiles[t] is None else tiles[t] + piece
        for t in range(TILES):
            result[pl.ds(c * per, per), :, t * LANES : (t + 1) * LANES] = (
                tiles[t].astype(jnp.bfloat16).reshape(per, message, LANES)
            )
        line = iota((span, LANES), 0) % message
        lse = jnp.where(lane_m // KVH == line, lse, 0.0)
        lse_out[pl.ds(c * per, per)] = jnp.sum(
            lse.reshape(per, message, LANES), axis=1, keepdims=True
        )

    def answer(c, low, high, arrival):
        def send_back(i, carry):
            pltpu.make_async_remote_copy(
                src_ref=result.at[i, :, pl.ds(low, high - low)],
                dst_ref=back.at[i, :, pl.ds(low, high - low)],
                send_sem=back_send_sem,
                recv_sem=back_sem.at[arrival],
                device_id=(lax.rem(me + i * (n - MIX), n),),
                device_id_type=MESH,
            ).start()
            return carry

        lax.fori_loop(jnp.maximum(c * per, 1), (c + 1) * per, send_back, 0)

    def answer_lse(i, c):
        pltpu.make_async_remote_copy(
            src_ref=lse_out.at[i],
            dst_ref=lse_back.at[i],
            send_sem=lse_send_sem,
            recv_sem=lse_sem,
            device_id=(lax.rem(me + i * (n - MIX), n),),
            device_id_type=MESH,
        ).start()
        return c

    def chunk(c, carry):
        until = EARLY + EACH * c
        lax.fori_loop(jnp.where(c == 0, 0, until - EACH), until, private_batch, 0)
        arrived = recv.at[pl.ds(c * per, per)]
        pltpu.make_async_copy(arrived, arrived, recv_sem.at[c]).wait()
        shared(c)
        lax.fori_loop(jnp.maximum(c * per, 1), (c + 1) * per, answer_lse, 0)

        @pl.when(c < CHUNKS - SPLIT)
        def _():
            answer(c, 0, KW, c)

        @pl.when(c >= CHUNKS - SPLIT)
        def _():
            answer(c, 0, CUT, c)

        return carry

    lax.fori_loop(0, CHUNKS, chunk, 0)
    for c in range(CHUNKS - SPLIT, CHUNKS):
        answer(c, CUT, KW, c + SPLIT)
    pltpu.make_async_copy(result.at[0], back.at[0], back_sem.at[0]).start()
    pltpu.make_async_copy(lse_out.at[0], lse_back.at[0], lse_sem).start()
    lax.fori_loop(EARLY + EACH * (CHUNKS - 1), rows // BATCH, private_batch, 0)

    others = send.at[pl.ds(1, n - 1)]
    pltpu.make_async_copy(others, others, send_sem).wait()
    pltpu.make_async_copy(w_v, w_v, load_sem.at[5]).wait()

    others = lse_out.at[pl.ds(1, n - 1)]
    pltpu.make_async_copy(others, others, lse_send_sem).wait()
    pltpu.make_async_copy(lse_back, lse_back, lse_sem).wait()
    used = GQ * SLOTS * KVH
    lse = lse_back[...].reshape(n, LANES)[:, :used]
    high = lse.astype(jnp.bfloat16).astype(jnp.float32)
    rest = lse - high
    middle = rest.astype(jnp.bfloat16).astype(jnp.float32)
    three = jnp.concatenate([high, middle, rest - middle, jnp.zeros_like(high)], axis=1)
    from_group = (group_col == (me + iota((rows, n), 1) * MIX) % n)
    from_group = from_group.astype(jnp.float32).astype(jnp.bfloat16)
    lines = dot(from_group, three.astype(jnp.bfloat16))
    lane3 = iota((rows, 4 * used), 1)
    mine = lane3 // KVH % SLOTS == rank_col
    lines = jnp.concatenate(
        [
            jnp.where(mine & (lane3 % used // (KVH * SLOTS) == j), lines, 0.0)
            for j in range(GQ)
        ],
        axis=0,
    )
    expand = of_head(iota((4 * used, KW), 1), iota((4 * used, KW), 0) % KVH)
    expand = expand.astype(jnp.float32).astype(jnp.bfloat16)
    prefix_lse = dot(lines.astype(jnp.bfloat16), expand)
    private_lse = own_lse[...]
    most = jnp.maximum(prefix_lse, private_lse)
    a = jnp.exp(prefix_lse - most)
    b = jnp.exp(private_lse - most)
    both = 1.0 / (a + b)
    own[...] = own[...] * (b * both)
    own_lse[...] = a * both

    def returned_rows(c, low, high, arrival):
        returned = back.at[pl.ds(c * per, per), :, pl.ds(low, high - low)]
        pltpu.make_async_copy(returned, returned, back_sem.at[arrival]).wait()
        arrived = back[pl.ds(c * per, per), :, low:high].reshape(span, high - low)
        return dot(pick_back[c], arrived)

    def gather(c, carry):
        spread[...] += returned_rows(c, 0, KW, c)
        return carry

    spread[...] = returned_rows(0, 0, KW, 0)
    lax.fori_loop(1, CHUNKS - SPLIT, gather, 0)
    width = 512
    for low, high, late in ((0, CUT, 0), (CUT, KW, SPLIT)):
        prefix_out = spread[:, low:high]
        for c in range(CHUNKS - SPLIT, CHUNKS):
            prefix_out = prefix_out + returned_rows(c, low, high, c + late)
        attended = own_lse[:, low:high] * prefix_out + own[:, low:high]
        attended = attended.astype(jnp.bfloat16)
        for t in range(o_ref.shape[1] // width):
            columns = slice(t * width, (t + 1) * width)
            part = None
            for j in range(GQ):
                term = dot(
                    attended[j * rows : (j + 1) * rows],
                    w_v[j * KW + low : j * KW + high, columns],
                )
                part = term if part is None else part + term
            if late:
                o_ref[:, columns] = (half[:, columns] + part).astype(jnp.bfloat16)
            else:
                half[:, columns] = part
    others = result.at[pl.ds(1, n - 1)]
    pltpu.make_async_copy(others, others, back_send_sem).wait()


def per_device(
    queries,
    prefix_keys,
    prefix_values,
    pool_keys,
    pool_values,
    page_table,
    private_length,
    group_ids,
    live_rows,
    out_weight,
):
    n = lax.axis_size("req")
    rows, width = queries.shape
    tokens = prefix_keys.shape[0]
    message = GQ * SLOTS
    bf16, f32 = jnp.bfloat16, jnp.float32
    vmem = pl.BlockSpec(memory_space=pltpu.VMEM)
    far = pl.BlockSpec(memory_space=pltpu.HBM)
    projected = pl.pallas_call(
        functools.partial(kernel, n, rows),
        out_shape=jax.ShapeDtypeStruct((rows, width), bf16),
        in_specs=[far] * 9,
        out_specs=vmem,
        scratch_shapes=[
            pltpu.SMEM(page_table.shape[::-1], jnp.int32),
            pltpu.SMEM(private_length.shape, jnp.int32),
            pltpu.VMEM((1, rows), jnp.int32),
            pltpu.VMEM(queries.shape, bf16),
            pltpu.VMEM(prefix_keys.shape, bf16),
            pltpu.VMEM(prefix_values.shape, bf16),
            pltpu.VMEM(pool_keys.shape, bf16),
            pltpu.VMEM(pool_values.shape, bf16),
            pltpu.VMEM(out_weight.shape, bf16),
            pltpu.VMEM((GQ * rows, KW), bf16),
            pltpu.VMEM((GQ * rows, KW), f32),
            pltpu.VMEM((KVH, tokens, 2 * LANES), bf16),
            pltpu.VMEM((KVH, tokens, 2 * LANES), bf16),
            pltpu.VMEM((n, message, KW), bf16),
            pltpu.VMEM((n, message, KW), bf16),
            pltpu.VMEM((n, message, KW), bf16),
            pltpu.VMEM((n, message, KW), bf16),
            pltpu.VMEM((n, 1, LANES), f32),
            pltpu.VMEM((n, 1, LANES), f32),
            pltpu.VMEM((TILES * BATCH * H, LANES), f32),
            pltpu.VMEM((BATCH * H, LANES), f32),
            pltpu.VMEM((GQ * rows, KW), f32),
            pltpu.VMEM((GQ * rows, KW), f32),
            pltpu.VMEM((CHUNKS, GQ * rows, n * message // CHUNKS), bf16),
            pltpu.VMEM((GQ * rows, KW), f32),
            pltpu.VMEM((rows, width), f32),
            pltpu.SemaphoreType.DMA((9,)),
            pltpu.SemaphoreType.DMA,
            pltpu.SemaphoreType.DMA((CHUNKS,)),
            pltpu.SemaphoreType.DMA,
            pltpu.SemaphoreType.DMA((CHUNKS + SPLIT,)),
            pltpu.SemaphoreType.DMA,
            pltpu.SemaphoreType.DMA,
        ],
        compiler_params=pltpu.CompilerParams(
            collective_id=0, has_side_effects=True, vmem_limit_bytes=48 << 20
        ),
    )(
        *(
            pltpu.with_memory_space_constraint(x, pltpu.HBM)
            for x in (
                page_table.T,
                private_length,
                group_ids.reshape(1, rows),
                queries,
                prefix_keys,
                prefix_values,
                pool_keys,
                pool_values,
                out_weight,
            )
        )
    )
    is_live = jnp.arange(rows, dtype=jnp.int32)[:, None] < live_rows[0]
    return jnp.where(is_live, projected, jnp.zeros_like(projected))


def solution(mesh):
    placed = (
        P("req", None),
        P("req", None),
        P("req", None),
        P("req", None, None),
        P("req", None, None),
        P("req", None),
        P("req"),
        P("req", None),
        P("req"),
        P(),
    )
    return jax.shard_map(
        per_device, mesh=mesh, in_specs=placed, out_specs=P("req", None), check_vma=False
    )
```
